1024 devices in a mesh: dp: 32 (over z), task: 8 (over y, core), mp: 4 (over x).
Axes of the slice: x: 4, y: 4, z: 32, core: 2. Of those that a mesh axis runs over, the one named last changes fastest.
Arguments:
- tokens: bfloat16 [49152, 2048], P(('dp', 'task')), may hold values from -6 to 6
- expert_ids: int32 [49152, 2], P(('dp', 'task')), may hold values from 0 to 31, all different within a row; in each aligned block of 192 rows (0 to 191, 192 to 383, ...) at most 15 rows name the same one
- gate_levels: int32 [49152, 2], P(('dp', 'task')), may hold values from 1 to 15
- expert_weight: bfloat16 [32, 2048, 4096], P('dp', None, 'mp'), may hold values from -0.125 to 0.125
- tower_weight: bfloat16 [8, 4096, 256], P(None, 'mp'), may hold values from -0.09375 to 0.09375
- tower_out: float32 [8, 256], P('task'), may hold values from -1.5 to 1.5
- cotangent: float32 [8, 49152], P('task', 'dp'), may hold values from -24 to 24
Outputs:
- predictions: float32 [8, 49152], P('task', 'dp')
- mix_grad: bfloat16 [49152, 4096], P(('dp', 'task'), 'mp')
The draws below stay inside these ranges and needn't reach their ends.
Inputs may be any that keep to these rules, and one draw needn't show every extreme that they name: `expert_ids`: each row names 2 different experts; in each aligned block of 192 rows (the rows of one device) no expert is named by more than 15 rows, and some expert reaches 15 in some block.
All inputs are finite; a program needn't handle non-finite values.
Results may differ from the reference program's by a relative error of at most 0.02.
Values may be sent and summed in bfloat16 or wider, within the bound.
No kernel may reach another device: no remote copies, remote signals or barrier semaphores. Data moves between devices by JAX's collectives and lax.ppermute only.
A program may use at most 64 MiB of HBM per device.

```python
import math
import jax
import jax.numpy as jnp
import numpy as np
from jax import lax

D = 2048
H = 4096
FT = 256
TOK_DEV = 192
TOP = 2
EXPERTS = 32
TASKS = 8
CAP = 15
TOKENS = 49152


def plant(array, rng, smallest, top_value):
    longest = array.shape.index(max(array.shape))
    spots = []
    for shift in (0, 1):
        where = [jax.random.randint(jax.random.fold_in(rng, axis), (), 0, length) for axis, length in enumerate(array.shape)]
        where[longest] = (where[longest] + shift) % array.shape[longest]
        spots.append(tuple(where))
    return array.at[spots[0]].set(smallest).at[spots[1]].set(top_value)


def shard_levels(own_key, dims, pieces, low, top_value):
    def one(dim, parts):
        steps = jax.random.uniform(jax.random.fold_in(jax.random.fold_in(own_key, 6), dim), (parts,), jnp.float32, low / len(pieces), top_value / len(pieces))
        return jnp.repeat(jnp.exp(steps), dims[dim] // parts).reshape((-1,) + (1,) * (len(dims) - dim - 1))

    loudness = one(*pieces[0])
    for cut in pieces[1:]:
        loudness = loudness * one(*cut)
    return loudness


def deal_out(stream_key, own, number, rows, count, top, bound, slope):
    order = jax.random.permutation(stream_key, count)
    packed, usual = load_shares(count, rows * top, bound, slope, True), load_shares(count, rows * top, bound, slope, False)
    places = jnp.arange(count)

    def named(sizes, turn):
        used = int((sizes > 0).sum())
        fixed = max(1, used // 4)
        moved = fixed + (places - fixed + turn * (used - fixed)) % max(1, count - fixed)
        return jnp.zeros((count,), jnp.int32).at[order[jnp.where(places < fixed, places, moved)]].set(jnp.asarray(sizes, jnp.int32))

    sizes = jnp.where(number % 4 == 0, named(packed, number // 4), named(usual, number - number // 4 - 1))
    mixed = jax.random.permutation(jax.random.fold_in(own, 3), count)
    source_of, sink = mixed[0:count // 2 * 2:2], mixed[1:count // 2 * 2:2]
    margin = jnp.minimum(sizes[source_of] - 1, bound - sizes[sink]) // 2
    margin = jnp.where((source_of == order[0]) | (sink == order[0]) | (sizes[sink] == 0), 0, jnp.maximum(margin, 0))
    moved = jax.random.randint(jax.random.fold_in(own, 4), (count // 2,), 0, 1 << 20) % (margin + 1)
    sizes = sizes.at[source_of].add(-moved).at[sink].add(moved)
    items = jnp.searchsorted(jnp.cumsum(sizes), jnp.arange(rows * top), side="right").astype(jnp.int32)
    grid = items.reshape(top, rows).T
    grid = grid[jax.random.permutation(jax.random.fold_in(own, 1), rows)]
    turn = jax.random.randint(jax.random.fold_in(own, 2), (rows, 1), 0, top)
    return jnp.take_along_axis(grid, (jnp.arange(top)[None, :] + turn) % top, axis=1)


def load_shares(amount, total, limit, skew, full):
    weights = [(1 << 20) // math.isqrt(rank ** skew) + 1 for rank in range(1, amount + 1)]
    largest = limit if full else min(limit, max(-(-total // amount), total * weights[0] // sum(weights)))
    least = 1 if total - largest >= amount - 1 else 0
    holding, spare = [largest] + [least] * (amount - 1), total - largest - least * (amount - 1)
    while spare > 0:
        free = [i for i in range(1, amount) if holding[i] < largest] or [i for i in range(1, amount) if holding[i] < limit]
        mass, remaining = sum([weights[i] for i in free]), spare
        for i in free:
            extra = min(limit - holding[i], max(1, remaining * weights[i] // mass), spare)
            holding[i] = holding[i] + extra
            spare = spare - extra
    return np.array(holding)


def scatter_about(own_key, extent, spread, limit, shards=(), held_as=jnp.bfloat16):
    drawn = jax.random.normal(own_key, extent, jnp.float32) * spread
    if len(shards) > 0:
        drawn = shard_levels(own_key, extent, shards, -0.22, 0.18) * drawn
    return jnp.clip(drawn, min=-limit, max=limit).astype(held_as)


def setup_inputs(seed: int = 0) -> dict:
    streams_of = jax.random.split(jax.random.key(seed), 8)
    tokens = scatter_about(streams_of[0], (TOKENS, D), 1.0, 6.0, ((0, 256),))
    expert_ids_keys = jax.random.split(jax.random.fold_in(streams_of[1], 1), TOKENS // TOK_DEV)
    expert_ids_turns = jax.random.permutation(jax.random.fold_in(streams_of[1], 3), TOKENS // TOK_DEV)
    expert_ids = jax.vmap(lambda own, number: deal_out(jax.random.fold_in(streams_of[1], 2), own, number, TOK_DEV, EXPERTS, TOP, CAP, 2))(expert_ids_keys, expert_ids_turns).reshape((TOKENS, TOP))
    gate_levels = plant(jax.random.randint(streams_of[2], (TOKENS, TOP), 1, 16), jax.random.fold_in(streams_of[2], 1), 1, 15).astype(jnp.int32)
    expert_weight = scatter_about(streams_of[3], (EXPERTS, D, H), D ** -0.5, 0.125, ((0, 32), (2, 4)))
    tower_weight = scatter_about(streams_of[4], (TASKS, H, FT), H ** -0.5, 0.09375, ((1, 4),))
    tower_out = scatter_about(streams_of[5], (TASKS, FT), 0.25, 1.5, ((0, 8),), jnp.float32)
    cotangent = scatter_about(streams_of[6], (TASKS, TOKENS), 4.0, 24.0, ((0, 8), (1, 32)), jnp.float32)
    return {"tokens": tokens, "expert_ids": expert_ids, "gate_levels": gate_levels, "expert_weight": expert_weight, "tower_weight": tower_weight, "tower_out": tower_out, "cotangent": cotangent}


def slot_table(expert_ids):
    blocks = TOKENS // TOK_DEV
    per_block = TOK_DEV * TOP
    ids = expert_ids.reshape(blocks, per_block).astype(jnp.int32)
    onehot = (ids[:, :, None] == jnp.arange(EXPERTS, dtype=jnp.int32)[None, None, :]).astype(jnp.int32)
    rank = jnp.cumsum(onehot, axis=1) - 1
    position = jnp.sum(onehot * rank, axis=2)
    block_ids = jnp.arange(blocks, dtype=jnp.int32)[:, None]
    dest = (ids * blocks + block_ids) * CAP + position
    route_ids = jnp.arange(blocks * per_block, dtype=jnp.int32).reshape(blocks, per_block)
    table = jnp.full((EXPERTS * blocks * CAP,), TOKENS * TOP, jnp.int32)
    return table.at[dest.reshape(-1)].set(route_ids.reshape(-1))


def reference(tokens, expert_ids, gate_levels, expert_weight, tower_weight, tower_out, cotangent):
    levels = gate_levels.astype(jnp.float32)
    gates = (levels / jnp.sum(levels, axis=1, keepdims=True)).reshape(-1)
    table = slot_table(expert_ids)
    slots = (TOKENS // TOK_DEV) * CAP

    def one_expert(acc, expert):
        routes = lax.dynamic_slice_in_dim(table, (expert * slots).astype(jnp.int32), slots)
        valid = routes < TOKENS * TOP
        safe_route = jnp.where(valid, routes, 0)
        owner = safe_route // TOP
        rows = tokens[owner]
        weight = lax.dynamic_index_in_dim(expert_weight, expert, 0, keepdims=False)
        hidden = jax.nn.silu(jnp.dot(rows, weight, preferred_element_type=jnp.float32)).astype(jnp.bfloat16)
        scale = jnp.where(valid, gates[safe_route], jnp.float32(0.0))
        target = jnp.where(valid, owner, TOKENS)
        acc = acc.at[target].add(scale[:, None] * hidden.astype(jnp.float32), mode="drop")
        return acc, None

    mix_acc, unused = lax.scan(one_expert, jnp.zeros((TOKENS, H), jnp.float32), jnp.arange(EXPERTS, dtype=jnp.int32))
    mix = mix_acc.astype(jnp.bfloat16)

    def one_tower(acc, inputs):
        weight, out_vec, cot = inputs
        z = jnp.dot(mix, weight, preferred_element_type=jnp.float32)
        sig = jax.nn.sigmoid(z)
        pred = jnp.dot(z * sig, out_vec, preferred_element_type=jnp.float32)
        dz = (cot[:, None] * out_vec[None, :] * sig * (1.0 + z * (1.0 - sig))).astype(jnp.bfloat16)
        term = jnp.dot(dz, weight.T, preferred_element_type=jnp.float32).astype(jnp.bfloat16)
        term = lax.optimization_barrier(term)
        return acc + term.astype(jnp.float32), pred

    grad_acc, predictions = lax.scan(one_tower, jnp.zeros((TOKENS, H), jnp.float32), (tower_weight, tower_out, cotangent))
    return predictions, grad_acc.astype(jnp.bfloat16)
```

```python
import functools

import jax
import jax.numpy as jnp
from jax import lax
from jax.experimental import pallas as pl
from jax.experimental.pallas import tpu as pltpu
from jax.sharding import PartitionSpec as P

F32 = jnp.float32
BF16 = jnp.bfloat16
VMEM = pl.BlockSpec(memory_space=pltpu.VMEM)
SMEM = pl.BlockSpec(memory_space=pltpu.SMEM)
LANES = (((1,), (1,)), ((), ()))
ROWS = (((0,), (0,)), ((), ()))


def slot_rows(ids_ref, experts, pitch):
    top, count = ids_ref.shape
    earlier = (
        lax.broadcasted_iota(jnp.int32, (count, count), 0)
        < lax.broadcasted_iota(jnp.int32, (count, count), 1)
    ).astype(F32).astype(BF16)
    names = lax.broadcasted_iota(jnp.int32, (experts, count), 0)
    seen = jnp.zeros((experts, 1), F32)
    slots = []
    for k in range(top):
        row = ids_ref[k : k + 1, :]
        hit = (names == row).astype(F32)
        before = jnp.dot(hit.astype(BF16), earlier, preferred_element_type=F32)
        rank = jnp.sum(hit * (before + seen), axis=0, keepdims=True)
        seen = seen + jnp.sum(hit, axis=1, keepdims=True)
        slots.append(row * pitch + rank.astype(jnp.int32))
    return slots


def dispatch_kernel(experts, pitch, col_ref, ids_ref, tok_ref, out_ref):
    slots = slot_rows(ids_ref, experts, pitch)
    count = ids_ref.shape[1]
    here = lax.broadcasted_iota(jnp.int32, (experts * pitch, count), 0)
    pick = functools.reduce(jnp.logical_or, [here == s for s in slots])
    pick = pick.astype(F32).astype(BF16)
    out_ref[...] = jnp.dot(pick, tok_ref[...], preferred_element_type=F32).astype(BF16)


def expert_kernel(n, me_ref, *refs):
    ins, (w_ref, tw_ref), outs, hid_ref = refs[:n], refs[n : n + 2], refs[n + 2 : -1], refs[-1]
    me = me_ref[0]
    depth = ins[0].shape[1]
    tile = tw_ref.shape[2]
    per = tw_ref.shape[0] // n

    @pl.loop(0, w_ref.shape[1] // tile)
    def _(c):
        cols = pl.ds(pl.multiple_of(c * tile, tile), tile)
        total = None
        for s in range(n):
            first = pl.multiple_of(lax.rem(me - s + n, n) * depth, depth)
            part = jnp.dot(ins[s][...], w_ref[pl.ds(first, depth), cols], preferred_element_type=F32)
            total = part if total is None else total + part
        hid_ref[:, cols] = (total / (1.0 + jnp.exp(-total))).astype(BF16)

    for s in range(n):
        to = lax.rem(me + s, n)
        for i in range(per):
            outs[s][:, i * tile : (i + 1) * tile] = jnp.dot(
                hid_ref[...], tw_ref[to * per + i], preferred_element_type=F32
            ).astype(BF16)


def combine_kernel(experts, pitch, ids_ref, lev_ref, back_ref, out_ref):
    slots = slot_rows(ids_ref, experts, pitch)
    levels = lev_ref[...].astype(F32)
    gates = levels / jnp.sum(levels, axis=0, keepdims=True)
    here = lax.broadcasted_iota(jnp.int32, (experts * pitch, ids_ref.shape[1]), 0)
    share = sum(jnp.where(here == s, gates[k : k + 1, :], 0.0) for k, s in enumerate(slots))
    high = share.astype(BF16)
    low = (share - high.astype(F32)).astype(BF16)
    rows = back_ref[...]
    z = lax.dot_general(high, rows, ROWS, preferred_element_type=F32)
    z = z + lax.dot_general(low, rows, ROWS, preferred_element_type=F32)
    out_ref[...] = z.astype(BF16)


def tower_kernel(n, me_ref, side_ref, *refs):
    ins, tw_ref, pred_ref, grad_ref, acc_ref = refs[:n], refs[n], refs[n + 1], refs[n + 2], refs[n + 3]
    me = me_ref[0]
    count = ins[0].shape[0]
    tile = tw_ref.shape[2]
    per = tw_ref.shape[0] // n
    cot = jnp.transpose(side_ref[:, :256])[:count]
    lane = lax.broadcasted_iota(jnp.int32, cot.shape, 1)
    for s in range(n):
        for i in range(per):
            t = lax.rem(me - s + n, n) * per + i
            z = ins[s][:, i * tile : (i + 1) * tile].astype(F32)
            out_vec = side_ref[pl.ds(t, 1), 256:]
            sig = 1.0 / (1.0 + jnp.exp(-z))
            pred_ref[pl.ds(t, 1), :] = lax.dot_general(
                out_vec, z * sig, LANES, precision=lax.Precision.HIGHEST, preferred_element_type=F32
            )
            c = jnp.sum(jnp.where(lane == t, cot, 0.0), axis=1, keepdims=True)
            dz = (c * out_vec * sig * (1.0 + z * (1.0 - sig))).astype(BF16)
            part = lax.dot_general(dz, tw_ref[t], LANES, preferred_element_type=F32)
            if s == 0 and i == 0:
                acc_ref[...] = part
            else:
                acc_ref[...] += part
    grad_ref[...] = acc_ref[...].astype(BF16)


def body(tokens, expert_ids, gate_levels, expert_weight, tower_weight, tower_out, cotangent):
    experts = lax.axis_size("dp")
    tasks = lax.axis_size("task")
    n = lax.axis_size("mp")
    count, top = expert_ids.shape
    width = tokens.shape[1]
    part = width // n
    towers, units, tile = tower_weight.shape
    cols = towers * tile // n
    cap = max(2, 5 * count * top // (4 * experts))
    pitch = -(-cap // 8) * 8
    rows = experts * pitch
    me = lax.axis_index("mp").astype(jnp.int32).reshape(1)
    ids = expert_ids.T
    levels = gate_levels.T

    side = jnp.concatenate(
        [
            jnp.pad(cotangent.reshape(tasks, count), ((0, 0), (0, 256 - count))),
            jnp.broadcast_to(tower_out, (tasks, tile)),
        ],
        axis=1,
    )
    side = lax.all_to_all(side, "task", split_axis=0, concat_axis=0, tiled=True)

    out = pl.pallas_call(
        functools.partial(dispatch_kernel, experts, pitch),
        out_shape=jax.ShapeDtypeStruct((rows, part), BF16),
        grid_spec=pltpu.PrefetchScalarGridSpec(
            num_scalar_prefetch=1,
            grid=(1,),
            in_specs=[
                pl.BlockSpec((top, count), lambda g, m: (0, 0)),
                pl.BlockSpec((count, part), lambda g, m: (0, m[0])),
            ],
            out_specs=pl.BlockSpec((rows, part), lambda g, m: (0, 0)),
        ),
        name="dispatch",
    )(me, ids, tokens)

    def over_dp(a):
        a = a.reshape(experts, pitch, a.shape[1])
        return lax.all_to_all(a, "dp", split_axis=0, concat_axis=0, tiled=True).reshape(rows, -1)

    def shift(a, s):
        return lax.ppermute(a, "mp", [(i, (i + s) % n) for i in range(n)])

    mine = over_dp(out)
    pieces = [mine] + [shift(mine, s) for s in range(1, n)]
    outs = pl.pallas_call(
        functools.partial(expert_kernel, n),
        out_shape=[jax.ShapeDtypeStruct((rows, cols), BF16)] * n,
        in_specs=[SMEM] + [VMEM] * (n + 2),
        out_specs=[VMEM] * n,
        scratch_shapes=[pltpu.VMEM((rows, units), BF16)],
        compiler_params=pltpu.CompilerParams(vmem_limit_bytes=40 << 20),
        cost_estimate=pl.CostEstimate(
            flops=2 * rows * units * (width + towers * tile),
            bytes_accessed=2 * units * (width + towers * tile),
            transcendentals=rows * units,
        ),
        name="expert",
    )(me, *pieces, expert_weight[0], tower_weight)
    total = sum([outs[0].astype(F32)] + [shift(outs[s], s).astype(F32) for s in range(1, n)])
    back = over_dp(total.astype(BF16))

    z = pl.pallas_call(
        functools.partial(combine_kernel, experts, pitch),
        out_shape=jax.ShapeDtypeStruct((count, cols), BF16),
        in_specs=[VMEM] * 3,
        out_specs=VMEM,
        name="combine",
    )(ids, levels, back)
    zs = [z] + [shift(z, s) for s in range(1, n)]

    pred, grad = pl.pallas_call(
        functools.partial(tower_kernel, n),
        out_shape=[
            jax.ShapeDtypeStruct((towers, count), F32),
            jax.ShapeDtypeStruct((count, units), BF16),
        ],
        in_specs=[SMEM] + [VMEM] * (n + 2),
        out_specs=[VMEM] * 2,
        scratch_shapes=[pltpu.VMEM((count, units), F32)],
        compiler_params=pltpu.CompilerParams(vmem_limit_bytes=40 << 20),
        name="tower",
    )(me, side, *zs, tower_weight)
    pred = lax.all_to_all(pred, "task", split_axis=0, concat_axis=0, tiled=True)
    return pred.reshape(1, tasks * count), grad


def solution(mesh):
    return jax.shard_map(
        body,
        mesh=mesh,
        in_specs=(
            P(("dp", "task"), None),
            P(("dp", "task"), None),
            P(("dp", "task"), None),
            P("dp", None, "mp"),
            P(None, "mp", None),
            P("task", None),
            P("task", "dp"),
        ),
        out_specs=(P("task", "dp"), P(("dp", "task"), "mp")),
        check_vma=False,
    )
```

```python
import functools

import jax
import jax.numpy as jnp
from jax import lax
from jax.experimental import pallas as pl
from jax.experimental.pallas import tpu as pltpu
from jax.sharding import PartitionSpec as P

F32 = jnp.float32
BF16 = jnp.bfloat16
VMEM = pl.BlockSpec(memory_space=pltpu.VMEM)
HBM = pl.BlockSpec(memory_space=pltpu.HBM)
SMEM = pl.BlockSpec(memory_space=pltpu.SMEM)
LANES = (((1,), (1,)), ((), ()))
ROWS = (((0,), (0,)), ((), ()))


def slot_rows(ids_ref, experts, pitch):
    top, count = ids_ref.shape
    earlier = (
        lax.broadcasted_iota(jnp.int32, (count, count), 0)
        < lax.broadcasted_iota(jnp.int32, (count, count), 1)
    ).astype(F32).astype(BF16)
    names = lax.broadcasted_iota(jnp.int32, (experts, count), 0)
    seen = jnp.zeros((experts, 1), F32)
    slots = []
    for k in range(top):
        row = ids_ref[k : k + 1, :]
        hit = (names == row).astype(F32)
        before = jnp.dot(hit.astype(BF16), earlier, preferred_element_type=F32)
        rank = jnp.sum(hit * (before + seen), axis=0, keepdims=True)
        seen = seen + jnp.sum(hit, axis=1, keepdims=True)
        slots.append(row * pitch + rank.astype(jnp.int32))
    return slots


def dispatch_kernel(experts, pitch, col_ref, ids_ref, tok_ref, out_ref):
    slots = slot_rows(ids_ref, experts, pitch)
    count = ids_ref.shape[1]
    here = lax.broadcasted_iota(jnp.int32, (experts * pitch, count), 0)
    pick = functools.reduce(jnp.logical_or, [here == s for s in slots])
    pick = pick.astype(F32).astype(BF16)
    out_ref[...] = jnp.dot(pick, tok_ref[...], preferred_element_type=F32).astype(BF16)


def expert_kernel(in_ref, w_hbm, tw_hbm, out_ref, w_ref, tw_ref, hid_ref, w_sem, tw_sem):
    n, _, depth = in_ref.shape
    towers, _, tile = tw_ref.shape
    tiles = w_ref.shape[0]
    per = towers // n

    def w_copy(c):
        cols = pl.ds(pl.multiple_of(c * tile, tile), tile)
        return pltpu.make_async_copy(w_hbm.at[0, :, cols], w_ref.at[c], w_sem.at[c])

    def tw_copy(t):
        return pltpu.make_async_copy(tw_hbm.at[t], tw_ref.at[t], tw_sem.at[t])

    for c in range(tiles):
        w_copy(c).start()
    for t in range(towers):
        tw_copy(t).start()

    @pl.loop(0, tiles)
    def _(c):
        w_copy(c).wait()
        total = None
        for j in range(n):
            part = jnp.dot(
                in_ref[j], w_ref[c, j * depth : (j + 1) * depth, :], preferred_element_type=F32
            )
            total = part if total is None else total + part
        cols = pl.ds(pl.multiple_of(c * tile, tile), tile)
        hid_ref[:, cols] = (total / (1.0 + jnp.exp(-total))).astype(BF16)

    for t in range(towers):
        tw_copy(t).wait()
        out_ref[t // per, :, (t % per) * tile : (t % per + 1) * tile] = jnp.dot(
            hid_ref[...], tw_ref[t], preferred_element_type=F32
        ).astype(BF16)


def combine_kernel(experts, pitch, ids_ref, lev_ref, back_ref, out_ref):
    slots = slot_rows(ids_ref, experts, pitch)
    levels = lev_ref[...].astype(F32)
    gates = levels / jnp.sum(levels, axis=0, keepdims=True)
    here = lax.broadcasted_iota(jnp.int32, (experts * pitch, ids_ref.shape[1]), 0)
    share = sum(jnp.where(here == s, gates[k : k + 1, :], 0.0) for k, s in enumerate(slots))
    high = share.astype(BF16)
    low = (share - high.astype(F32)).astype(BF16)
    rows = back_ref[...]
    z = lax.dot_general(high, rows, ROWS, preferred_element_type=F32)
    z = z + lax.dot_general(low, rows, ROWS, preferred_element_type=F32)
    out_ref[...] = z.astype(BF16)


def from_tower(side_ref, me, t):
    return side_ref[pl.ds(jnp.bitwise_xor(me, t), 1), pl.ds(me, 1), :].reshape(1, -1)


def predict_kernel(towers, me_ref, side_ref, z_ref, pred_ref):
    me = me_ref[0]
    n, count, cols = z_ref.shape
    per = towers // n
    tile = cols // per
    for t in range(towers):
        z = z_ref[t // per, :, (t % per) * tile : (t % per + 1) * tile].astype(F32)
        out_vec = from_tower(side_ref, me, t)[:, -tile:]
        pred_ref[t : t + 1, :] = lax.dot_general(
            out_vec,
            z / (1.0 + jnp.exp(-z)),
            LANES,
            precision=lax.Precision.HIGHEST,
            preferred_element_type=F32,
        )


def gradient_kernel(me_ref, side_ref, z_ref, tw_hbm, grad_ref, tw_ref, acc_ref, tw_sem):
    me = me_ref[0]
    n, count, cols = z_ref.shape
    towers, _, tile = tw_ref.shape
    per = towers // n
    copies = [pltpu.make_async_copy(tw_hbm.at[t], tw_ref.at[t], tw_sem.at[t]) for t in range(towers)]
    for copy in copies:
        copy.start()
    sides = [from_tower(side_ref, me, t) for t in range(towers)]
    cot = jnp.transpose(jnp.concatenate([v[:, :-tile] for v in sides], axis=0))[:count]
    for t in range(towers):
        z = z_ref[t // per, :, (t % per) * tile : (t % per + 1) * tile].astype(F32)
        sig = 1.0 / (1.0 + jnp.exp(-z))
        dz = cot[:, t : t + 1] * sides[t][:, -tile:] * sig * (1.0 + z * (1.0 - sig))
        copies[t].wait()
        part = lax.dot_general(dz.astype(BF16), tw_ref[t], LANES, preferred_element_type=F32)
        if t == 0:
            acc_ref[...] = part
        elif t < towers - 1:
            acc_ref[...] += part
        else:
            grad_ref[...] = (acc_ref[...] + part).astype(BF16)


def body(tokens, expert_ids, gate_levels, expert_weight, tower_weight, tower_out, cotangent):
    experts = lax.axis_size("dp")
    tasks = lax.axis_size("task")
    n = lax.axis_size("mp")
    count, top = expert_ids.shape
    width = tokens.shape[1]
    part = width // n
    towers, units, tile = tower_weight.shape
    cols = towers * tile // n
    cap = max(2, 5 * count * top // (4 * experts))
    pitch = -(-cap // 8) * 8
    rows = experts * pitch
    me = lax.axis_index("mp").astype(jnp.int32).reshape(1)
    ids = expert_ids.T
    levels = gate_levels.T

    side = jnp.concatenate(
        [
            jnp.pad(cotangent.reshape(tasks, count), ((0, 0), (0, 256 - count))),
            jnp.broadcast_to(tower_out, (tasks, tile)),
        ],
        axis=1,
    )
    side = side[None]
    for bit in (1, 2, 4):
        other = lax.ppermute(side, "task", [(i, i ^ bit) for i in range(tasks)])
        side = jnp.concatenate([side, other], axis=0)

    out = pl.pallas_call(
        functools.partial(dispatch_kernel, experts, pitch),
        out_shape=jax.ShapeDtypeStruct((rows, part), BF16),
        grid_spec=pltpu.PrefetchScalarGridSpec(
            num_scalar_prefetch=1,
            grid=(1,),
            in_specs=[
                pl.BlockSpec((top, count), lambda g, m: (0, 0)),
                pl.BlockSpec((count, part), lambda g, m: (0, m[0])),
            ],
            out_specs=pl.BlockSpec((rows, part), lambda g, m: (0, 0)),
        ),
        name="dispatch",
    )(me, ids, tokens)

    def over_dp(a):
        a = a.reshape(experts, pitch, a.shape[1])
        return lax.all_to_all(a, "dp", split_axis=0, concat_axis=0, tiled=True).reshape(rows, -1)

    def over_mp(a):
        return lax.all_to_all(a, "mp", split_axis=0, concat_axis=0, tiled=True)

    def spread(a):
        return over_mp(jnp.broadcast_to(a[None], (n,) + a.shape))

    outs = pl.pallas_call(
        expert_kernel,
        out_shape=jax.ShapeDtypeStruct((n, rows, cols), BF16),
        in_specs=[VMEM, HBM, HBM],
        out_specs=VMEM,
        scratch_shapes=[
            pltpu.VMEM((units // tile, width, tile), BF16),
            pltpu.VMEM((towers, units, tile), BF16),
            pltpu.VMEM((rows, units), BF16),
            pltpu.SemaphoreType.DMA((units // tile,)),
            pltpu.SemaphoreType.DMA((towers,)),
        ],
        compiler_params=pltpu.CompilerParams(vmem_limit_bytes=50 << 20),
        cost_estimate=pl.CostEstimate(
            flops=2 * rows * units * (width + towers * tile),
            bytes_accessed=2 * units * (width + towers * tile),
            transcendentals=rows * units,
        ),
        name="expert",
    )(spread(over_dp(out)), expert_weight, tower_weight)
    total = jnp.sum(over_mp(outs).astype(F32), axis=0)
    back, side = lax.optimization_barrier((over_dp(total.astype(BF16)), side))

    z = pl.pallas_call(
        functools.partial(combine_kernel, experts, pitch),
        out_shape=jax.ShapeDtypeStruct((count, cols), BF16),
        in_specs=[VMEM] * 3,
        out_specs=VMEM,
        compiler_params=pltpu.CompilerParams(vmem_limit_bytes=16 << 20),
        name="combine",
    )(ids, levels, back)
    zs = spread(z)

    task = lax.axis_index("task").astype(jnp.int32).reshape(1)
    pred = pl.pallas_call(
        functools.partial(predict_kernel, towers),
        out_shape=jax.ShapeDtypeStruct((towers, count), F32),
        in_specs=[SMEM, VMEM, VMEM],
        out_specs=VMEM,
        compiler_params=pltpu.CompilerParams(vmem_limit_bytes=16 << 20),
        name="predict",
    )(task, side, zs)
    grad = pl.pallas_call(
        gradient_kernel,
        out_shape=jax.ShapeDtypeStruct((count, units), BF16),
        in_specs=[SMEM, VMEM, VMEM, HBM],
        out_specs=VMEM,
        scratch_shapes=[
            pltpu.VMEM((towers, units, tile), BF16),
            pltpu.VMEM((count, units), F32),
            pltpu.SemaphoreType.DMA((towers,)),
        ],
        compiler_params=pltpu.CompilerParams(vmem_limit_bytes=54 << 20),
        cost_estimate=pl.CostEstimate(
            flops=2 * count * units * towers * tile,
            bytes_accessed=2 * units * towers * tile,
            transcendentals=count * towers * tile,
        ),
        name="gradient",
    )(task, side, zs, tower_weight)
    pred = lax.all_to_all(pred, "task", split_axis=0, concat_axis=0, tiled=True)
    return pred.reshape(1, tasks * count), grad


def solution(mesh):
    return jax.shard_map(
        body,
        mesh=mesh,
        in_specs=(
            P(("dp", "task"), None),
            P(("dp", "task"), None),
            P(("dp", "task"), None),
            P("dp", None, "mp"),
            P(None, "mp", None),
            P("task", None),
            P("task", "dp"),
        ),
        out_specs=(P("task", "dp"), P(("dp", "task"), "mp")),
        check_vma=False,
    )
```

```python
import functools

import jax
import jax.numpy as jnp
from jax import lax
from jax.experimental import pallas as pl
from jax.experimental.pallas import tpu as pltpu
from jax.sharding import PartitionSpec as P

F32 = jnp.float32
BF16 = jnp.bfloat16
VMEM = pl.BlockSpec(memory_space=pltpu.VMEM)
HBM = pl.BlockSpec(memory_space=pltpu.HBM)
SMEM = pl.BlockSpec(memory_space=pltpu.SMEM)
LANES = (((1,), (1,)), ((), ()))
ROWS = (((0,), (0,)), ((), ()))


def slot_rows(ids_ref, experts, pitch):
    top, count = ids_ref.shape
    earlier = (
        lax.broadcasted_iota(jnp.int32, (count, count), 0)
        < lax.broadcasted_iota(jnp.int32, (count, count), 1)
    ).astype(F32).astype(BF16)
    names = lax.broadcasted_iota(jnp.int32, (experts, count), 0)
    seen = jnp.zeros((experts, 1), F32)
    slots = []
    for k in range(top):
        row = ids_ref[k : k + 1, :]
        hit = (names == row).astype(F32)
        before = jnp.dot(hit.astype(BF16), earlier, preferred_element_type=F32)
        rank = jnp.sum(hit * (before + seen), axis=0, keepdims=True)
        seen = seen + jnp.sum(hit, axis=1, keepdims=True)
        slots.append(row * pitch + rank.astype(jnp.int32))
    return slots


def dispatch_kernel(experts, pitch, col_ref, ids_ref, tok_ref, out_ref):
    slots = slot_rows(ids_ref, experts, pitch)
    count = ids_ref.shape[1]
    here = lax.broadcasted_iota(jnp.int32, (experts * pitch, count), 0)
    pick = functools.reduce(jnp.logical_or, [here == s for s in slots])
    pick = pick.astype(F32).astype(BF16)
    out_ref[...] = jnp.dot(pick, tok_ref[...], preferred_element_type=F32).astype(BF16)


def expert_kernel(in_hbm, w_hbm, tw_hbm, out_ref, in_ref, w_ref, tw_ref, acc_ref, hid_ref, in_sem, w_sem, tw_sem):
    n, _, depth = in_ref.shape
    towers, _, tile = tw_ref.shape
    per = towers // n
    in_copies = [pltpu.make_async_copy(in_hbm.at[j], in_ref.at[j], in_sem.at[j]) for j in range(n)]
    w_copies = [
        pltpu.make_async_copy(w_hbm.at[0, pl.ds(j * depth, depth)], w_ref.at[j], w_sem.at[j])
        for j in range(n)
    ]
    tw_copies = [pltpu.make_async_copy(tw_hbm.at[t], tw_ref.at[t], tw_sem.at[t]) for t in range(towers)]
    for j in range(n):
        in_copies[j].start()
        w_copies[j].start()
    for copy in tw_copies:
        copy.start()

    for j in range(n):
        in_copies[j].wait()
        w_copies[j].wait()

        @pl.loop(0, w_ref.shape[2] // tile)
        def _(c):
            cols = pl.ds(pl.multiple_of(c * tile, tile), tile)
            total = jnp.dot(in_ref[j], w_ref[j, :, cols], preferred_element_type=F32)
            if j > 0:
                total = total + acc_ref[:, cols]
            if j < n - 1:
                acc_ref[:, cols] = total
            else:
                hid_ref[:, cols] = (total / (1.0 + jnp.exp(-total))).astype(BF16)

    for t in range(towers):
        tw_copies[t].wait()
        out_ref[t // per, :, (t % per) * tile : (t % per + 1) * tile] = jnp.dot(
            hid_ref[...], tw_ref[t], preferred_element_type=F32
        ).astype(BF16)


def combine_kernel(experts, pitch, ids_ref, lev_ref, back_ref, out_ref):
    slots = slot_rows(ids_ref, experts, pitch)
    levels = lev_ref[...].astype(F32)
    gates = levels / jnp.sum(levels, axis=0, keepdims=True)
    here = lax.broadcasted_iota(jnp.int32, (experts * pitch, ids_ref.shape[1]), 0)
    share = sum(jnp.where(here == s, gates[k : k + 1, :], 0.0) for k, s in enumerate(slots))
    high = share.astype(BF16)
    low = (share - high.astype(F32)).astype(BF16)
    rows = back_ref[...]
    z = lax.dot_general(high, rows, ROWS, preferred_element_type=F32)
    z = z + lax.dot_general(low, rows, ROWS, preferred_element_type=F32)
    for j in range(out_ref.shape[0]):
        out_ref[j] = z.astype(BF16)


def from_tower(side_ref, me, t):
    return side_ref[pl.ds(jnp.bitwise_xor(me, t), 1), pl.ds(me, 1), :].reshape(1, -1)


def predict_kernel(towers, me_ref, side_ref, z_ref, pred_ref):
    me = me_ref[0]
    n, count, cols = z_ref.shape
    per = towers // n
    tile = cols // per
    for t in range(towers):
        z = z_ref[t // per, :, (t % per) * tile : (t % per + 1) * tile].astype(F32)
        out_vec = from_tower(side_ref, me, t)[:, -tile:]
        pred_ref[t] = lax.dot_general(
            out_vec,
            z / (1.0 + jnp.exp(-z)),
            LANES,
            precision=lax.Precision.HIGHEST,
            preferred_element_type=F32,
        )


def gradient_kernel(me_ref, side_ref, z_ref, tw_hbm, grad_ref, tw_ref, acc_ref, tw_sem):
    me = me_ref[0]
    n, count, cols = z_ref.shape
    towers, _, tile = tw_ref.shape
    per = towers // n
    copies = [pltpu.make_async_copy(tw_hbm.at[t], tw_ref.at[t], tw_sem.at[t]) for t in range(towers)]
    for copy in copies:
        copy.start()
    sides = [from_tower(side_ref, me, t) for t in range(towers)]
    cot = jnp.transpose(jnp.concatenate([v[:, :-tile] for v in sides], axis=0))[:count]
    for t in range(towers):
        z = z_ref[t // per, :, (t % per) * tile : (t % per + 1) * tile].astype(F32)
        sig = 1.0 / (1.0 + jnp.exp(-z))
        dz = cot[:, t : t + 1] * sides[t][:, -tile:] * sig * (1.0 + z * (1.0 - sig))
        copies[t].wait()
        part = lax.dot_general(dz.astype(BF16), tw_ref[t], LANES, preferred_element_type=F32)
        if t == 0:
            acc_ref[...] = part
        elif t < towers - 1:
            acc_ref[...] += part
        else:
            grad_ref[...] = (acc_ref[...] + part).astype(BF16)


def body(tokens, expert_ids, gate_levels, expert_weight, tower_weight, tower_out, cotangent):
    experts = lax.axis_size("dp")
    tasks = lax.axis_size("task")
    n = lax.axis_size("mp")
    count, top = expert_ids.shape
    width = tokens.shape[1]
    part = width // n
    towers, units, tile = tower_weight.shape
    cols = towers * tile // n
    cap = max(2, 5 * count * top // (4 * experts))
    pitch = -(-cap // 8) * 8
    rows = experts * pitch
    me = lax.axis_index("mp").astype(jnp.int32).reshape(1)
    ids = expert_ids.T
    levels = gate_levels.T

    side = jnp.concatenate(
        [
            jnp.pad(cotangent.reshape(tasks, count), ((0, 0), (0, 256 - count))),
            jnp.broadcast_to(tower_out, (tasks, tile)),
        ],
        axis=1,
    )
    side = side[None]
    for bit in (1, 2, 4):
        other = lax.ppermute(side, "task", [(i, i ^ bit) for i in range(tasks)])
        side = jnp.concatenate([side, other], axis=0)

    out = pl.pallas_call(
        functools.partial(dispatch_kernel, experts, pitch),
        out_shape=jax.ShapeDtypeStruct((rows, part), BF16),
        grid_spec=pltpu.PrefetchScalarGridSpec(
            num_scalar_prefetch=1,
            grid=(1,),
            in_specs=[
                pl.BlockSpec((top, count), lambda g, m: (0, 0)),
                pl.BlockSpec((count, part), lambda g, m: (0, m[0])),
            ],
            out_specs=pl.BlockSpec((rows, part), lambda g, m: (0, 0)),
        ),
        name="dispatch",
    )(me, ids, tokens)

    def over_dp(a):
        a = a.reshape(experts, pitch, a.shape[1])
        return lax.all_to_all(a, "dp", split_axis=0, concat_axis=0, tiled=True).reshape(rows, -1)

    def over_mp(a):
        return lax.all_to_all(a, "mp", split_axis=0, concat_axis=0, tiled=True)

    def spread(a):
        return over_mp(jnp.broadcast_to(a[None], (n,) + a.shape))

    outs = pl.pallas_call(
        expert_kernel,
        out_shape=jax.ShapeDtypeStruct((n, rows, cols), BF16),
        in_specs=[HBM] * 3,
        out_specs=VMEM,
        scratch_shapes=[
            pltpu.VMEM((n, rows, part), BF16),
            pltpu.VMEM((n, part, units), BF16),
            pltpu.VMEM((towers, units, tile), BF16),
            pltpu.VMEM((rows, units), F32),
            pltpu.VMEM((rows, units), BF16),
            pltpu.SemaphoreType.DMA((n,)),
            pltpu.SemaphoreType.DMA((n,)),
            pltpu.SemaphoreType.DMA((towers,)),
        ],
        compiler_params=pltpu.CompilerParams(vmem_limit_bytes=50 << 20),
        cost_estimate=pl.CostEstimate(
            flops=2 * rows * units * (width + towers * tile),
            bytes_accessed=2 * units * (width + towers * tile),
            transcendentals=rows * units,
        ),
        name="expert",
    )(spread(over_dp(out)), expert_weight, tower_weight)
    total = jnp.sum(over_mp(outs).astype(F32), axis=0)
    back, side = lax.optimization_barrier((over_dp(total.astype(BF16)), side))

    z = pl.pallas_call(
        functools.partial(combine_kernel, experts, pitch),
        out_shape=jax.ShapeDtypeStruct((n, count, cols), BF16),
        in_specs=[VMEM] * 3,
        out_specs=VMEM,
        compiler_params=pltpu.CompilerParams(vmem_limit_bytes=16 << 20),
        name="combine",
    )(ids, levels, back)
    zs = over_mp(z)

    task = lax.axis_index("task").astype(jnp.int32).reshape(1)
    pred = pl.pallas_call(
        functools.partial(predict_kernel, towers),
        out_shape=jax.ShapeDtypeStruct((towers, 1, count), F32),
        in_specs=[SMEM, VMEM, VMEM],
        out_specs=VMEM,
        compiler_params=pltpu.CompilerParams(vmem_limit_bytes=16 << 20),
        name="predict",
    )(task, side, zs)
    grad = pl.pallas_call(
        gradient_kernel,
        out_shape=jax.ShapeDtypeStruct((count, units), BF16),
        in_specs=[SMEM, VMEM, VMEM, HBM],
        out_specs=VMEM,
        scratch_shapes=[
            pltpu.VMEM((towers, units, tile), BF16),
            pltpu.VMEM((count, units), F32),
            pltpu.SemaphoreType.DMA((towers,)),
        ],
        compiler_params=pltpu.CompilerParams(vmem_limit_bytes=54 << 20),
        cost_estimate=pl.CostEstimate(
            flops=2 * count * units * towers * tile,
            bytes_accessed=2 * units * towers * tile,
            transcendentals=count * towers * tile,
        ),
        name="gradient",
    )(task, side, zs, tower_weight)
    pred = lax.all_to_all(pred, "task", split_axis=0, concat_axis=0, tiled=True)
    return pred.reshape(1, tasks * count), grad


def solution(mesh):
    return jax.shard_map(
        body,
        mesh=mesh,
        in_specs=(
            P(("dp", "task"), None),
            P(("dp", "task"), None),
            P(("dp", "task"), None),
            P("dp", None, "mp"),
            P(None, "mp", None),
            P("task", None),
            P("task", "dp"),
        ),
        out_specs=(P("task", "dp"), P(("dp", "task"), "mp")),
        check_vma=False,
    )
```

```python
import functools

import jax
import jax.numpy as jnp
from jax import lax
from jax.experimental import pallas as pl
from jax.experimental.pallas import tpu as pltpu
from jax.sharding import PartitionSpec as P

F32 = jnp.float32
BF16 = jnp.bfloat16
VMEM = pl.BlockSpec(memory_space=pltpu.VMEM)
HBM = pl.BlockSpec(memory_space=pltpu.HBM)
SMEM = pl.BlockSpec(memory_space=pltpu.SMEM)
LANES = (((1,), (1,)), ((), ()))
ROWS = (((0,), (0,)), ((), ()))


def slot_rows(ids_ref, experts, pitch):
    top, count = ids_ref.shape
    earlier = (
        lax.broadcasted_iota(jnp.int32, (count, count), 0)
        < lax.broadcasted_iota(jnp.int32, (count, count), 1)
    ).astype(F32).astype(BF16)
    names = lax.broadcasted_iota(jnp.int32, (experts, count), 0)
    seen = jnp.zeros((experts, 1), F32)
    slots = []
    for k in range(top):
        row = ids_ref[k : k + 1, :]
        hit = (names == row).astype(F32)
        before = jnp.dot(hit.astype(BF16), earlier, preferred_element_type=F32)
        rank = jnp.sum(hit * (before + seen), axis=0, keepdims=True)
        seen = seen + jnp.sum(hit, axis=1, keepdims=True)
        slots.append(row * pitch + rank.astype(jnp.int32))
    return slots


def dispatch_kernel(experts, pitch, col_ref, ids_ref, tok_ref, out_ref):
    slots = slot_rows(ids_ref, experts, pitch)
    count = ids_ref.shape[1]
    here = lax.broadcasted_iota(jnp.int32, (experts * pitch, count), 0)
    pick = functools.reduce(jnp.logical_or, [here == s for s in slots])
    pick = pick.astype(F32).astype(BF16)
    out_ref[...] = jnp.dot(pick, tok_ref[...], preferred_element_type=F32).astype(BF16)


def expert_kernel(in_hbm, w_hbm, tw_hbm, out_ref, in_ref, w_ref, tw_ref, acc_ref, hid_ref, in_sem, w_sem, tw_sem):
    n, _, depth = in_ref.shape
    towers, _, tile = tw_ref.shape
    per = towers // n
    in_copies = [pltpu.make_async_copy(in_hbm.at[j], in_ref.at[j], in_sem.at[j]) for j in range(n)]
    w_copies = [
        pltpu.make_async_copy(w_hbm.at[0, pl.ds(j * depth, depth)], w_ref.at[j], w_sem.at[j])
        for j in range(n)
    ]
    tw_copies = [pltpu.make_async_copy(tw_hbm.at[t], tw_ref.at[t], tw_sem.at[t]) for t in range(towers)]
    steps = [[in_copies[j], w_copies[j]] for j in range(n)] + [[copy] for copy in tw_copies]
    for step in steps[:2]:
        for copy in step:
            copy.start()

    def arrive(i):
        for copy in steps[i]:
            copy.wait()
        for copy in sum(steps[i + 2 : i + 3], []):
            copy.start()

    for j in range(n):
        arrive(j)

        @pl.loop(0, w_ref.shape[2] // tile)
        def _(c):
            cols = pl.ds(pl.multiple_of(c * tile, tile), tile)
            total = jnp.dot(in_ref[j], w_ref[j, :, cols], preferred_element_type=F32)
            if j > 0:
                total = total + acc_ref[:, cols]
            if j < n - 1:
                acc_ref[:, cols] = total
            else:
                hid_ref[:, cols] = (total / (1.0 + jnp.exp(-total))).astype(BF16)

    for t in range(towers):
        arrive(n + t)
        out_ref[t // per, :, (t % per) * tile : (t % per + 1) * tile] = jnp.dot(
            hid_ref[...], tw_ref[t], preferred_element_type=F32
        ).astype(BF16)


def combine_kernel(experts, pitch, ids_ref, lev_ref, back_ref, out_ref):
    slots = slot_rows(ids_ref, experts, pitch)
    levels = lev_ref[...].astype(F32)
    gates = levels / jnp.sum(levels, axis=0, keepdims=True)
    here = lax.broadcasted_iota(jnp.int32, (experts * pitch, ids_ref.shape[1]), 0)
    share = sum(jnp.where(here == s, gates[k : k + 1, :], 0.0) for k, s in enumerate(slots))
    high = share.astype(BF16)
    low = (share - high.astype(F32)).astype(BF16)
    rows = back_ref[...]
    z = lax.dot_general(high, rows, ROWS, preferred_element_type=F32)
    z = z + lax.dot_general(low, rows, ROWS, preferred_element_type=F32)
    for j in range(out_ref.shape[0]):
        out_ref[j] = z.astype(BF16)


def from_tower(side_ref, me, t):
    return side_ref[pl.ds(jnp.bitwise_xor(me, t), 1), pl.ds(me, 1), :].reshape(1, -1)


def predict_kernel(towers, me_ref, side_ref, z_ref, pred_ref):
    me = me_ref[0]
    n, count, cols = z_ref.shape
    per = towers // n
    tile = cols // per
    for t in range(towers):
        z = z_ref[t // per, :, (t % per) * tile : (t % per + 1) * tile].astype(F32)
        out_vec = from_tower(side_ref, me, t)[:, -tile:]
        pred_ref[t] = lax.dot_general(
            out_vec,
            z / (1.0 + jnp.exp(-z)),
            LANES,
            precision=lax.Precision.HIGHEST,
            preferred_element_type=F32,
        )


def gradient_kernel(me_ref, side_ref, z_ref, tw_hbm, grad_ref, tw_ref, acc_ref, tw_sem):
    me = me_ref[0]
    n, count, cols = z_ref.shape
    towers, _, tile = tw_ref.shape
    per = towers // n
    copies = [pltpu.make_async_copy(tw_hbm.at[t], tw_ref.at[t], tw_sem.at[t]) for t in range(towers)]
    for copy in copies[:2]:
        copy.start()
    sides = [from_tower(side_ref, me, t) for t in range(towers)]
    cot = jnp.transpose(jnp.concatenate([v[:, :-tile] for v in sides], axis=0))[:count]
    for t in range(towers):
        z = z_ref[t // per, :, (t % per) * tile : (t % per + 1) * tile].astype(F32)
        sig = 1.0 / (1.0 + jnp.exp(-z))
        dz = cot[:, t : t + 1] * sides[t][:, -tile:] * sig * (1.0 + z * (1.0 - sig))
        copies[t].wait()
        if t + 2 < towers:
            copies[t + 2].start()
        part = lax.dot_general(dz.astype(BF16), tw_ref[t], LANES, preferred_element_type=F32)
        if t == 0:
            acc_ref[...] = part
        elif t < towers - 1:
            acc_ref[...] += part
        else:
            grad_ref[...] = (acc_ref[...] + part).astype(BF16)


def body(tokens, expert_ids, gate_levels, expert_weight, tower_weight, tower_out, cotangent):
    experts = lax.axis_size("dp")
    tasks = lax.axis_size("task")
    n = lax.axis_size("mp")
    count, top = expert_ids.shape
    width = tokens.shape[1]
    part = width // n
    towers, units, tile = tower_weight.shape
    cols = towers * tile // n
    cap = max(2, 5 * count * top // (4 * experts))
    rows = experts * cap
    me = lax.axis_index("mp").astype(jnp.int32).reshape(1)
    ids = expert_ids.T
    levels = gate_levels.T

    side = jnp.concatenate(
        [
            jnp.pad(cotangent.reshape(tasks, count), ((0, 0), (0, 256 - count))),
            jnp.broadcast_to(tower_out, (tasks, tile)),
        ],
        axis=1,
    )
    side = side[None]
    for bit in (1, 2, 4):
        other = lax.ppermute(side, "task", [(i, i ^ bit) for i in range(tasks)])
        side = jnp.concatenate([side, other], axis=0)

    out = pl.pallas_call(
        functools.partial(dispatch_kernel, experts, cap),
        out_shape=jax.ShapeDtypeStruct((rows, part), BF16),
        grid_spec=pltpu.PrefetchScalarGridSpec(
            num_scalar_prefetch=1,
            grid=(1,),
            in_specs=[
                pl.BlockSpec((top, count), lambda g, m: (0, 0)),
                pl.BlockSpec((count, part), lambda g, m: (0, m[0])),
            ],
            out_specs=pl.BlockSpec((rows, part), lambda g, m: (0, 0)),
        ),
        name="dispatch",
    )(me, ids, tokens)

    def over_dp(a):
        a = a.reshape(experts, cap, 2, a.shape[1] // 2)
        return lax.all_to_all(a, "dp", split_axis=0, concat_axis=0, tiled=True).reshape(rows, -1)

    def over_mp(a):
        return lax.all_to_all(a, "mp", split_axis=0, concat_axis=0, tiled=True)

    def spread(a):
        return over_mp(jnp.broadcast_to(a[None], (n,) + a.shape))

    outs = pl.pallas_call(
        expert_kernel,
        out_shape=jax.ShapeDtypeStruct((n, rows, cols), BF16),
        in_specs=[HBM] * 3,
        out_specs=VMEM,
        scratch_shapes=[
            pltpu.VMEM((n, rows, part), BF16),
            pltpu.VMEM((n, part, units), BF16),
            pltpu.VMEM((towers, units, tile), BF16),
            pltpu.VMEM((rows, units), F32),
            pltpu.VMEM((rows, units), BF16),
            pltpu.SemaphoreType.DMA((n,)),
            pltpu.SemaphoreType.DMA((n,)),
            pltpu.SemaphoreType.DMA((towers,)),
        ],
        compiler_params=pltpu.CompilerParams(vmem_limit_bytes=50 << 20),
        cost_estimate=pl.CostEstimate(
            flops=2 * rows * units * (width + towers * tile),
            bytes_accessed=2 * units * (width + towers * tile),
            transcendentals=rows * units,
        ),
        name="expert",
    )(spread(over_dp(out)), expert_weight, tower_weight)
    total = jnp.sum(over_mp(outs).astype(F32), axis=0)
    back, side = lax.optimization_barrier((over_dp(total.astype(BF16)), side))

    z = pl.pallas_call(
        functools.partial(combine_kernel, experts, cap),
        out_shape=jax.ShapeDtypeStruct((n, count, cols), BF16),
        in_specs=[VMEM] * 3,
        out_specs=VMEM,
        compiler_params=pltpu.CompilerParams(vmem_limit_bytes=16 << 20),
        name="combine",
    )(ids, levels, back)
    zs = over_mp(z)

    task = lax.axis_index("task").astype(jnp.int32).reshape(1)
    pred = pl.pallas_call(
        functools.partial(predict_kernel, towers),
        out_shape=jax.ShapeDtypeStruct((towers, 1, count), F32),
        in_specs=[SMEM, VMEM, VMEM],
        out_specs=VMEM,
        compiler_params=pltpu.CompilerParams(vmem_limit_bytes=16 << 20),
        name="predict",
    )(task, side, zs)
    grad = pl.pallas_call(
        gradient_kernel,
        out_shape=jax.ShapeDtypeStruct((count, units), BF16),
        in_specs=[SMEM, VMEM, VMEM, HBM],
        out_specs=VMEM,
        scratch_shapes=[
            pltpu.VMEM((towers, units, tile), BF16),
            pltpu.VMEM((count, units), F32),
            pltpu.SemaphoreType.DMA((towers,)),
        ],
        compiler_params=pltpu.CompilerParams(vmem_limit_bytes=54 << 20),
        cost_estimate=pl.CostEstimate(
            flops=2 * count * units * towers * tile,
            bytes_accessed=2 * units * towers * tile,
            transcendentals=count * towers * tile,
        ),
        name="gradient",
    )(task, side, zs, tower_weight)
    pred = lax.all_to_all(pred, "task", split_axis=0, concat_axis=0, tiled=True)
    return pred.reshape(1, tasks * count), grad


def solution(mesh):
    return jax.shard_map(
        body,
        mesh=mesh,
        in_specs=(
            P(("dp", "task"), None),
            P(("dp", "task"), None),
            P(("dp", "task"), None),
            P("dp", None, "mp"),
            P(None, "mp", None),
            P("task", None),
            P("task", "dp"),
        ),
        out_specs=(P("task", "dp"), P(("dp", "task"), "mp")),
        check_vma=False,
    )
```

```python
import functools

import jax
import jax.numpy as jnp
from jax import lax
from jax.experimental import pallas as pl
from jax.experimental.pallas import tpu as pltpu
from jax.sharding import PartitionSpec as P

F32 = jnp.float32
BF16 = jnp.bfloat16
VMEM = pl.BlockSpec(memory_space=pltpu.VMEM)
SMEM = pl.BlockSpec(memory_space=pltpu.SMEM)
LANES = (((1,), (1,)), ((), ()))
ROWS = (((0,), (0,)), ((), ()))


def slot_rows(ids_ref, experts, pitch):
    top, count = ids_ref.shape
    earlier = (
        lax.broadcasted_iota(jnp.int32, (count, count), 0)
        < lax.broadcasted_iota(jnp.int32, (count, count), 1)
    ).astype(F32).astype(BF16)
    names = lax.broadcasted_iota(jnp.int32, (experts, count), 0)
    seen = jnp.zeros((experts, 1), F32)
    slots = []
    for k in range(top):
        row = ids_ref[k : k + 1, :]
        hit = (names == row).astype(F32)
        before = jnp.dot(hit.astype(BF16), earlier, preferred_element_type=F32)
        rank = jnp.sum(hit * (before + seen), axis=0, keepdims=True)
        seen = seen + jnp.sum(hit, axis=1, keepdims=True)
        slots.append(row * pitch + rank.astype(jnp.int32))
    return slots


def dispatch_kernel(experts, pitch, col_ref, ids_ref, tok_ref, out_ref):
    slots = slot_rows(ids_ref, experts, pitch)
    count = ids_ref.shape[1]
    here = lax.broadcasted_iota(jnp.int32, (experts * pitch, count), 0)
    pick = functools.reduce(jnp.logical_or, [here == s for s in slots])
    pick = pick.astype(F32).astype(BF16)
    out_ref[...] = jnp.dot(pick, tok_ref[...], preferred_element_type=F32).astype(BF16)


def units_kernel(in_ref, w_ref, hid_ref):
    n, _, depth = in_ref.shape
    tile = 256

    @pl.loop(0, w_ref.shape[2] // tile)
    def _(c):
        cols = pl.ds(pl.multiple_of(c * tile, tile), tile)
        total = None
        for j in range(n):
            part = jnp.dot(
                in_ref[j], w_ref[0, j * depth : (j + 1) * depth, cols], preferred_element_type=F32
            )
            total = part if total is None else total + part
        hid_ref[:, cols] = (total / (1.0 + jnp.exp(-total))).astype(BF16)


def layers_kernel(hid_ref, tw_ref, out_ref):
    towers, _, tile = tw_ref.shape
    per = towers // out_ref.shape[0]
    for t in range(towers):
        out_ref[t // per, :, (t % per) * tile : (t % per + 1) * tile] = jnp.dot(
            hid_ref[...], tw_ref[t], preferred_element_type=F32
        ).astype(BF16)


def combine_kernel(experts, pitch, ids_ref, lev_ref, back_ref, out_ref):
    slots = slot_rows(ids_ref, experts, pitch)
    levels = lev_ref[...].astype(F32)
    gates = levels / jnp.sum(levels, axis=0, keepdims=True)
    here = lax.broadcasted_iota(jnp.int32, (experts * pitch, ids_ref.shape[1]), 0)
    share = sum(jnp.where(here == s, gates[k : k + 1, :], 0.0) for k, s in enumerate(slots))
    high = share.astype(BF16)
    low = (share - high.astype(F32)).astype(BF16)
    rows = back_ref[...]
    z = lax.dot_general(high, rows, ROWS, preferred_element_type=F32)
    z = z + lax.dot_general(low, rows, ROWS, preferred_element_type=F32)
    for j in range(out_ref.shape[0]):
        out_ref[j] = z.astype(BF16)


def from_tower(side_ref, me, t):
    return side_ref[pl.ds(jnp.bitwise_xor(me, t), 1), pl.ds(me, 1), :].reshape(1, -1)


def predict_kernel(towers, me_ref, side_ref, z_ref, pred_ref):
    me = me_ref[0]
    n, count, cols = z_ref.shape
    per = towers // n
    tile = cols // per
    for t in range(towers):
        z = z_ref[t // per, :, (t % per) * tile : (t % per + 1) * tile].astype(F32)
        out_vec = from_tower(side_ref, me, t)[:, -tile:]
        pred_ref[t] = lax.dot_general(
            out_vec,
            z / (1.0 + jnp.exp(-z)),
            LANES,
            precision=lax.Precision.HIGHEST,
            preferred_element_type=F32,
        )


def gradient_kernel(me_ref, side_ref, z_ref, tw_ref, grad_ref, acc_ref):
    me = me_ref[0]
    n, count, cols = z_ref.shape
    towers, _, tile = tw_ref.shape
    per = towers // n
    sides = [from_tower(side_ref, me, t) for t in range(towers)]
    cot = jnp.transpose(jnp.concatenate([v[:, :-tile] for v in sides], axis=0))[:count]
    for t in range(towers):
        z = z_ref[t // per, :, (t % per) * tile : (t % per + 1) * tile].astype(F32)
        sig = 1.0 / (1.0 + jnp.exp(-z))
        dz = cot[:, t : t + 1] * sides[t][:, -tile:] * sig * (1.0 + z * (1.0 - sig))
        part = lax.dot_general(dz.astype(BF16), tw_ref[t], LANES, preferred_element_type=F32)
        if t == 0:
            acc_ref[...] = part
        elif t < towers - 1:
            acc_ref[...] += part
        else:
            grad_ref[...] = (acc_ref[...] + part).astype(BF16)


def body(tokens, expert_ids, gate_levels, expert_weight, tower_weight, tower_out, cotangent):
    experts = lax.axis_size("dp")
    tasks = lax.axis_size("task")
    n = lax.axis_size("mp")
    count, top = expert_ids.shape
    width = tokens.shape[1]
    part = width // n
    towers, units, tile = tower_weight.shape
    cols = towers * tile // n
    cap = max(2, 5 * count * top // (4 * experts))
    rows = experts * cap
    me = lax.axis_index("mp").astype(jnp.int32).reshape(1)
    ids = expert_ids.T
    levels = gate_levels.T

    side = jnp.concatenate(
        [
            jnp.pad(cotangent.reshape(tasks, count), ((0, 0), (0, 256 - count))),
            jnp.broadcast_to(tower_out, (tasks, tile)),
        ],
        axis=1,
    )
    side = side[None]
    for bit in (1, 2, 4):
        other = lax.ppermute(side, "task", [(i, i ^ bit) for i in range(tasks)])
        side = jnp.concatenate([side, other], axis=0)

    out = pl.pallas_call(
        functools.partial(dispatch_kernel, experts, cap),
        out_shape=jax.ShapeDtypeStruct((rows, part), BF16),
        grid_spec=pltpu.PrefetchScalarGridSpec(
            num_scalar_prefetch=1,
            grid=(1,),
            in_specs=[
                pl.BlockSpec((top, count), lambda g, m: (0, 0)),
                pl.BlockSpec((count, part), lambda g, m: (0, m[0])),
            ],
            out_specs=pl.BlockSpec((rows, part), lambda g, m: (0, 0)),
        ),
        name="dispatch",
    )(me, ids, tokens)

    def over_dp(a):
        a = a.reshape(experts, cap, 2, a.shape[1] // 2)
        return lax.all_to_all(a, "dp", split_axis=0, concat_axis=0, tiled=True).reshape(rows, -1)

    def over_mp(a):
        return lax.all_to_all(a, "mp", split_axis=0, concat_axis=0, tiled=True)

    def spread(a):
        return over_mp(jnp.broadcast_to(a[None], (n,) + a.shape))

    hidden = pl.pallas_call(
        units_kernel,
        out_shape=jax.ShapeDtypeStruct((rows, units), BF16),
        in_specs=[VMEM] * 2,
        out_specs=VMEM,
        compiler_params=pltpu.CompilerParams(vmem_limit_bytes=24 << 20),
        cost_estimate=pl.CostEstimate(
            flops=2 * rows * units * width,
            bytes_accessed=2 * (units * width + rows * (units + width)),
            transcendentals=rows * units,
        ),
        name="units",
    )(spread(over_dp(out)), expert_weight)
    outs = pl.pallas_call(
        layers_kernel,
        out_shape=jax.ShapeDtypeStruct((n, rows, cols), BF16),
        in_specs=[VMEM] * 2,
        out_specs=VMEM,
        compiler_params=pltpu.CompilerParams(vmem_limit_bytes=24 << 20),
        cost_estimate=pl.CostEstimate(
            flops=2 * rows * units * towers * tile,
            bytes_accessed=2 * (units * towers * tile + rows * (units + towers * tile)),
            transcendentals=0,
        ),
        name="layers",
    )(hidden, tower_weight)
    total = jnp.sum(over_mp(outs).astype(F32), axis=0)
    back, side = lax.optimization_barrier((over_dp(total.astype(BF16)), side))

    z = pl.pallas_call(
        functools.partial(combine_kernel, experts, cap),
        out_shape=jax.ShapeDtypeStruct((n, count, cols), BF16),
        in_specs=[VMEM] * 3,
        out_specs=VMEM,
        compiler_params=pltpu.CompilerParams(vmem_limit_bytes=16 << 20),
        name="combine",
    )(ids, levels, back)
    zs = over_mp(z)

    task = lax.axis_index("task").astype(jnp.int32).reshape(1)
    pred = pl.pallas_call(
        functools.partial(predict_kernel, towers),
        out_shape=jax.ShapeDtypeStruct((towers, 1, count), F32),
        in_specs=[SMEM, VMEM, VMEM],
        out_specs=VMEM,
        compiler_params=pltpu.CompilerParams(vmem_limit_bytes=16 << 20),
        name="predict",
    )(task, side, zs)
    grad = pl.pallas_call(
        gradient_kernel,
        out_shape=jax.ShapeDtypeStruct((count, units), BF16),
        in_specs=[SMEM] + [VMEM] * 3,
        out_specs=VMEM,
        scratch_shapes=[pltpu.VMEM((count, units), F32)],
        compiler_params=pltpu.CompilerParams(vmem_limit_bytes=24 << 20),
        cost_estimate=pl.CostEstimate(
            flops=2 * count * units * towers * tile,
            bytes_accessed=2 * units * towers * tile,
            transcendentals=count * towers * tile,
        ),
        name="gradient",
    )(task, side, zs, tower_weight)
    pred = lax.all_to_all(pred, "task", split_axis=0, concat_axis=0, tiled=True)
    return pred.reshape(1, tasks * count), grad


def solution(mesh):
    return jax.shard_map(
        body,
        mesh=mesh,
        in_specs=(
            P(("dp", "task"), None),
            P(("dp", "task"), None),
            P(("dp", "task"), None),
            P("dp", None, "mp"),
            P(None, "mp", None),
            P("task", None),
            P("task", "dp"),
        ),
        out_specs=(P("task", "dp"), P(("dp", "task"), "mp")),
        check_vma=False,
    )
```

```python
import functools

import jax
import jax.numpy as jnp
from jax import lax
from jax.experimental import pallas as pl
from jax.experimental.pallas import tpu as pltpu
from jax.sharding import PartitionSpec as P

F32 = jnp.float32
BF16 = jnp.bfloat16
VMEM = pl.BlockSpec(memory_space=pltpu.VMEM)
SMEM = pl.BlockSpec(memory_space=pltpu.SMEM)
LANES = (((1,), (1,)), ((), ()))
ROWS = (((0,), (0,)), ((), ()))


def slot_rows(ids_ref, experts, pitch):
    top, count = ids_ref.shape
    earlier = (
        lax.broadcasted_iota(jnp.int32, (count, count), 0)
        < lax.broadcasted_iota(jnp.int32, (count, count), 1)
    ).astype(F32).astype(BF16)
    names = lax.broadcasted_iota(jnp.int32, (experts, count), 0)
    seen = jnp.zeros((experts, 1), F32)
    slots = []
    for k in range(top):
        row = ids_ref[k : k + 1, :]
        hit = (names == row).astype(F32)
        before = jnp.dot(hit.astype(BF16), earlier, preferred_element_type=F32)
        rank = jnp.sum(hit * (before + seen), axis=0, keepdims=True)
        seen = seen + jnp.sum(hit, axis=1, keepdims=True)
        slots.append(row * pitch + rank.astype(jnp.int32))
    return slots


def dispatch_kernel(experts, pitch, col_ref, ids_ref, tok_ref, out_ref):
    slots = slot_rows(ids_ref, experts, pitch)
    count = ids_ref.shape[1]
    here = lax.broadcasted_iota(jnp.int32, (experts * pitch, count), 0)
    pick = functools.reduce(jnp.logical_or, [here == s for s in slots])
    pick = pick.astype(F32).astype(BF16)
    out_ref[...] = jnp.dot(pick, tok_ref[...], preferred_element_type=F32).astype(BF16)


def units_kernel(in_ref, w_ref, hid_ref):
    n, _, depth = in_ref.shape
    tile = 256

    @pl.loop(0, w_ref.shape[2] // tile)
    def _(c):
        cols = pl.ds(pl.multiple_of(c * tile, tile), tile)
        total = None
        for j in range(n):
            part = jnp.dot(
                in_ref[j], w_ref[0, j * depth : (j + 1) * depth, cols], preferred_element_type=F32
            )
            total = part if total is None else total + part
        hid_ref[:, cols] = (total / (1.0 + jnp.exp(-total))).astype(BF16)


def layers_kernel(hid_ref, tw_ref, out_ref):
    towers, _, tile = tw_ref.shape
    per = towers // out_ref.shape[0]
    for t in range(towers):
        out_ref[t // per, :, (t % per) * tile : (t % per + 1) * tile] = jnp.dot(
            hid_ref[...], tw_ref[t], preferred_element_type=F32
        ).astype(BF16)


def combine_kernel(experts, pitch, ids_ref, lev_ref, back_ref, out_ref):
    slots = slot_rows(ids_ref, experts, pitch)
    levels = lev_ref[...].astype(F32)
    gates = levels / jnp.sum(levels, axis=0, keepdims=True)
    here = lax.broadcasted_iota(jnp.int32, (experts * pitch, ids_ref.shape[1]), 0)
    share = sum(jnp.where(here == s, gates[k : k + 1, :], 0.0) for k, s in enumerate(slots))
    high = share.astype(BF16)
    low = (share - high.astype(F32)).astype(BF16)
    rows = back_ref[...]
    z = lax.dot_general(high, rows, ROWS, preferred_element_type=F32)
    z = z + lax.dot_general(low, rows, ROWS, preferred_element_type=F32)
    for j in range(out_ref.shape[0]):
        out_ref[j] = z.astype(BF16)


def from_tower(side_ref, me, t):
    return side_ref[pl.ds(jnp.bitwise_xor(me, t), 1), pl.ds(me, 1), :].reshape(1, -1)


def predict_kernel(towers, me_ref, side_ref, z_ref, pred_ref):
    me = me_ref[0]
    n, count, cols = z_ref.shape
    per = towers // n
    tile = cols // per
    lane = lax.broadcasted_iota(jnp.int32, (count, 128), 1)
    sums = jnp.zeros((count, 128), F32)
    for t in range(towers):
        z = z_ref[t // per, :, (t % per) * tile : (t % per + 1) * tile].astype(F32)
        out_vec = from_tower(side_ref, me, t)[:, -tile:]
        pred = jnp.sum(z / (1.0 + jnp.exp(-z)) * out_vec, axis=1, keepdims=True)
        sums = jnp.where(lane == t, pred, sums)
    sums = jnp.concatenate([sums, jnp.zeros((-count % 128, 128), F32)], axis=0)
    rows = jnp.transpose(sums)
    for t in range(towers):
        pred_ref[t] = rows[t : t + 1, :count]


def gradient_kernel(me_ref, side_ref, z_ref, tw_ref, grad_ref, acc_ref):
    me = me_ref[0]
    n, count, cols = z_ref.shape
    towers, _, tile = tw_ref.shape
    per = towers // n
    sides = [from_tower(side_ref, me, t) for t in range(towers)]
    cot = jnp.transpose(jnp.concatenate([v[:, :-tile] for v in sides], axis=0))[:count]
    for t in range(towers):
        z = z_ref[t // per, :, (t % per) * tile : (t % per + 1) * tile].astype(F32)
        sig = 1.0 / (1.0 + jnp.exp(-z))
        dz = cot[:, t : t + 1] * sides[t][:, -tile:] * sig * (1.0 + z * (1.0 - sig))
        part = lax.dot_general(dz.astype(BF16), tw_ref[t], LANES, preferred_element_type=F32)
        if t == 0:
            acc_ref[...] = part
        elif t < towers - 1:
            acc_ref[...] += part
        else:
            grad_ref[...] = (acc_ref[...] + part).astype(BF16)


def body(tokens, expert_ids, gate_levels, expert_weight, tower_weight, tower_out, cotangent):
    experts = lax.axis_size("dp")
    tasks = lax.axis_size("task")
    n = lax.axis_size("mp")
    count, top = expert_ids.shape
    width = tokens.shape[1]
    part = width // n
    towers, units, tile = tower_weight.shape
    cols = towers * tile // n
    cap = max(2, 5 * count * top // (4 * experts))
    rows = experts * cap
    me = lax.axis_index("mp").astype(jnp.int32).reshape(1)
    ids = expert_ids.T
    levels = gate_levels.T

    side = jnp.concatenate(
        [
            jnp.pad(cotangent.reshape(tasks, count), ((0, 0), (0, 256 - count))),
            jnp.broadcast_to(tower_out, (tasks, tile)),
        ],
        axis=1,
    )
    side = side[None]
    for bit in (1, 2, 4):
        other = lax.ppermute(side, "task", [(i, i ^ bit) for i in range(tasks)])
        side = jnp.concatenate([side, other], axis=0)

    out = pl.pallas_call(
        functools.partial(dispatch_kernel, experts, cap),
        out_shape=jax.ShapeDtypeStruct((rows, part), BF16),
        grid_spec=pltpu.PrefetchScalarGridSpec(
            num_scalar_prefetch=1,
            grid=(1,),
            in_specs=[
                pl.BlockSpec((top, count), lambda g, m: (0, 0)),
                pl.BlockSpec((count, part), lambda g, m: (0, m[0])),
            ],
            out_specs=pl.BlockSpec((rows, part), lambda g, m: (0, 0)),
        ),
        name="dispatch",
    )(me, ids, tokens)

    def over_dp(a):
        a = a.reshape(experts, cap, 2, a.shape[1] // 2)
        return lax.all_to_all(a, "dp", split_axis=0, concat_axis=0, tiled=True).reshape(rows, -1)

    def over_mp(a):
        return lax.all_to_all(a, "mp", split_axis=0, concat_axis=0, tiled=True)

    def spread(a):
        return over_mp(jnp.broadcast_to(a[None], (n,) + a.shape))

    hidden = pl.pallas_call(
        units_kernel,
        out_shape=jax.ShapeDtypeStruct((rows, units), BF16),
        in_specs=[VMEM] * 2,
        out_specs=VMEM,
        compiler_params=pltpu.CompilerParams(vmem_limit_bytes=24 << 20),
        cost_estimate=pl.CostEstimate(
            flops=2 * rows * units * width,
            bytes_accessed=2 * (units * width + rows * (units + width)),
            transcendentals=rows * units,
        ),
        name="units",
    )(spread(over_dp(out)), expert_weight)
    outs = pl.pallas_call(
        layers_kernel,
        out_shape=jax.ShapeDtypeStruct((n, rows, cols), BF16),
        in_specs=[VMEM] * 2,
        out_specs=VMEM,
        compiler_params=pltpu.CompilerParams(vmem_limit_bytes=24 << 20),
        cost_estimate=pl.CostEstimate(
            flops=2 * rows * units * towers * tile,
            bytes_accessed=2 * (units * towers * tile + rows * (units + towers * tile)),
            transcendentals=0,
        ),
        name="layers",
    )(hidden, tower_weight)
    total = jnp.sum(over_mp(outs).astype(F32), axis=0)
    task = lax.axis_index("task").astype(jnp.int32).reshape(1)
    back, side, task = lax.optimization_barrier((over_dp(total.astype(BF16)), side, task))

    z = pl.pallas_call(
        functools.partial(combine_kernel, experts, cap),
        out_shape=jax.ShapeDtypeStruct((n, count, cols), BF16),
        in_specs=[VMEM] * 3,
        out_specs=VMEM,
        compiler_params=pltpu.CompilerParams(vmem_limit_bytes=16 << 20),
        name="combine",
    )(ids, levels, back)
    zs = over_mp(z)

    pred = pl.pallas_call(
        functools.partial(predict_kernel, towers),
        out_shape=jax.ShapeDtypeStruct((towers, 1, count), F32),
        in_specs=[SMEM, VMEM, VMEM],
        out_specs=VMEM,
        compiler_params=pltpu.CompilerParams(vmem_limit_bytes=16 << 20),
        name="predict",
    )(task, side, zs)
    grad = pl.pallas_call(
        gradient_kernel,
        out_shape=jax.ShapeDtypeStruct((count, units), BF16),
        in_specs=[SMEM] + [VMEM] * 3,
        out_specs=VMEM,
        scratch_shapes=[pltpu.VMEM((count, units), F32)],
        compiler_params=pltpu.CompilerParams(vmem_limit_bytes=24 << 20),
        cost_estimate=pl.CostEstimate(
            flops=2 * count * units * towers * tile,
            bytes_accessed=2 * units * towers * tile,
            transcendentals=count * towers * tile,
        ),
        name="gradient",
    )(task, side, zs, tower_weight)
    pred = lax.all_to_all(pred, "task", split_axis=0, concat_axis=0, tiled=True)
    return pred.reshape(1, tasks * count), grad


def solution(mesh):
    return jax.shard_map(
        body,
        mesh=mesh,
        in_specs=(
            P(("dp", "task"), None),
            P(("dp", "task"), None),
            P(("dp", "task"), None),
            P("dp", None, "mp"),
            P(None, "mp", None),
            P("task", None),
            P("task", "dp"),
        ),
        out_specs=(P("task", "dp"), P(("dp", "task"), "mp")),
        check_vma=False,
    )
```

```python
import functools

import jax
import jax.numpy as jnp
from jax import lax
from jax.experimental import pallas as pl
from jax.experimental.pallas import tpu as pltpu
from jax.sharding import PartitionSpec as P

F32 = jnp.float32
BF16 = jnp.bfloat16
VMEM = pl.BlockSpec(memory_space=pltpu.VMEM)
SMEM = pl.BlockSpec(memory_space=pltpu.SMEM)
LANES = (((1,), (1,)), ((), ()))
ROWS = (((0,), (0,)), ((), ()))


def slot_rows(ids_ref, experts, pitch):
    top, count = ids_ref.shape
    earlier = (
        lax.broadcasted_iota(jnp.int32, (count, count), 0)
        < lax.broadcasted_iota(jnp.int32, (count, count), 1)
    ).astype(F32).astype(BF16)
    names = lax.broadcasted_iota(jnp.int32, (experts, count), 0)
    seen = jnp.zeros((experts, 1), F32)
    slots = []
    for k in range(top):
        row = ids_ref[k : k + 1, :]
        hit = (names == row).astype(F32)
        before = jnp.dot(hit.astype(BF16), earlier, preferred_element_type=F32)
        rank = jnp.sum(hit * (before + seen), axis=0, keepdims=True)
        seen = seen + jnp.sum(hit, axis=1, keepdims=True)
        slots.append(row * pitch + rank.astype(jnp.int32))
    return slots


def by_tiles(rows, out_ref):
    groups, halves, high, wide = out_ref.shape
    for h in range(halves):
        out_ref[:, h] = rows[:, h * wide : (h + 1) * wide].reshape(groups, high, wide).astype(BF16)


def sum_kernel(in_ref, out_ref):
    by_tiles(sum(in_ref[j].astype(F32) for j in range(in_ref.shape[0])), out_ref)


def dispatch_kernel(experts, pitch, col_ref, ids_ref, tok_ref, out_ref):
    slots = slot_rows(ids_ref, experts, pitch)
    count = ids_ref.shape[1]
    here = lax.broadcasted_iota(jnp.int32, (experts * pitch, count), 0)
    pick = functools.reduce(jnp.logical_or, [here == s for s in slots])
    pick = pick.astype(F32).astype(BF16)
    by_tiles(jnp.dot(pick, tok_ref[...], preferred_element_type=F32), out_ref)


def units_kernel(in_ref, w_ref, hid_ref):
    n, _, depth = in_ref.shape
    tile = 256

    @pl.loop(0, w_ref.shape[2] // tile)
    def _(c):
        cols = pl.ds(pl.multiple_of(c * tile, tile), tile)
        total = None
        for j in range(n):
            part = jnp.dot(
                in_ref[j], w_ref[0, j * depth : (j + 1) * depth, cols], preferred_element_type=F32
            )
            total = part if total is None else total + part
        hid_ref[:, cols] = (total / (1.0 + jnp.exp(-total))).astype(BF16)


def layers_kernel(hid_ref, tw_ref, out_ref):
    towers, _, tile = tw_ref.shape
    per = towers // out_ref.shape[0]
    for t in range(towers):
        out_ref[t // per, :, (t % per) * tile : (t % per + 1) * tile] = jnp.dot(
            hid_ref[...], tw_ref[t], preferred_element_type=F32
        ).astype(BF16)


def combine_kernel(experts, pitch, ids_ref, lev_ref, back_ref, out_ref):
    slots = slot_rows(ids_ref, experts, pitch)
    levels = lev_ref[...].astype(F32)
    gates = levels / jnp.sum(levels, axis=0, keepdims=True)
    here = lax.broadcasted_iota(jnp.int32, (experts * pitch, ids_ref.shape[1]), 0)
    share = sum(jnp.where(here == s, gates[k : k + 1, :], 0.0) for k, s in enumerate(slots))
    high = share.astype(BF16)
    low = (share - high.astype(F32)).astype(BF16)
    rows = back_ref[...]
    z = lax.dot_general(high, rows, ROWS, preferred_element_type=F32)
    z = z + lax.dot_general(low, rows, ROWS, preferred_element_type=F32)
    for j in range(out_ref.shape[0]):
        out_ref[j] = z.astype(BF16)


def from_tower(side_ref, me, t):
    return side_ref[pl.ds(jnp.bitwise_xor(me, t), 1), pl.ds(me, 1), :].reshape(1, -1)


def predict_kernel(towers, me_ref, side_ref, z_ref, pred_ref):
    me = me_ref[0]
    n, count, cols = z_ref.shape
    per = towers // n
    tile = cols // per
    lane = lax.broadcasted_iota(jnp.int32, (count, 128), 1)
    sums = jnp.zeros((count, 128), F32)
    for t in range(towers):
        z = z_ref[t // per, :, (t % per) * tile : (t % per + 1) * tile].astype(F32)
        out_vec = from_tower(side_ref, me, t)[:, -tile:]
        pred = jnp.sum(z / (1.0 + jnp.exp(-z)) * out_vec, axis=1, keepdims=True)
        sums = jnp.where(lane == t, pred, sums)
    sums = jnp.concatenate([sums, jnp.zeros((-count % 128, 128), F32)], axis=0)
    rows = jnp.transpose(sums)
    for t in range(towers):
        pred_ref[t] = rows[t : t + 1, :count]


def gradient_kernel(me_ref, side_ref, z_ref, tw_ref, grad_ref, acc_ref):
    me = me_ref[0]
    n, count, cols = z_ref.shape
    towers, _, tile = tw_ref.shape
    per = towers // n
    sides = [from_tower(side_ref, me, t) for t in range(towers)]
    cot = jnp.transpose(jnp.concatenate([v[:, :-tile] for v in sides], axis=0))[:count]
    for t in range(towers):
        z = z_ref[t // per, :, (t % per) * tile : (t % per + 1) * tile].astype(F32)
        sig = 1.0 / (1.0 + jnp.exp(-z))
        dz = cot[:, t : t + 1] * sides[t][:, -tile:] * sig * (1.0 + z * (1.0 - sig))
        part = lax.dot_general(dz.astype(BF16), tw_ref[t], LANES, preferred_element_type=F32)
        if t == 0:
            acc_ref[...] = part
        elif t < towers - 1:
            acc_ref[...] += part
        else:
            grad_ref[...] = (acc_ref[...] + part).astype(BF16)


def body(tokens, expert_ids, gate_levels, expert_weight, tower_weight, tower_out, cotangent):
    experts = lax.axis_size("dp")
    tasks = lax.axis_size("task")
    n = lax.axis_size("mp")
    count, top = expert_ids.shape
    width = tokens.shape[1]
    part = width // n
    towers, units, tile = tower_weight.shape
    cols = towers * tile // n
    cap = max(2, 5 * count * top // (4 * experts))
    rows = experts * cap
    me = lax.axis_index("mp").astype(jnp.int32).reshape(1)
    ids = expert_ids.T
    levels = gate_levels.T

    side = jnp.concatenate(
        [
            jnp.pad(cotangent.reshape(tasks, count), ((0, 0), (0, 256 - count))),
            jnp.broadcast_to(tower_out, (tasks, tile)),
        ],
        axis=1,
    )
    side = side[None]
    for bit in (1, 2, 4):
        other = lax.ppermute(side, "task", [(i, i ^ bit) for i in range(tasks)])
        side = jnp.concatenate([side, other], axis=0)

    out = pl.pallas_call(
        functools.partial(dispatch_kernel, experts, cap),
        out_shape=jax.ShapeDtypeStruct((rows // 8, 2, 8, part // 2), BF16),
        grid_spec=pltpu.PrefetchScalarGridSpec(
            num_scalar_prefetch=1,
            grid=(1,),
            in_specs=[
                pl.BlockSpec((top, count), lambda g, m: (0, 0)),
                pl.BlockSpec((count, part), lambda g, m: (0, m[0])),
            ],
            out_specs=pl.BlockSpec((rows // 8, 2, 8, part // 2), lambda g, m: (0, 0, 0, 0)),
        ),
        name="dispatch",
    )(me, ids, tokens)

    def over_dp(a):
        a = a.transpose(0, 2, 1, 3).reshape(experts, cap, 2, a.shape[3])
        return lax.all_to_all(a, "dp", split_axis=0, concat_axis=0, tiled=True).reshape(rows, -1)

    def over_mp(a):
        return lax.all_to_all(a, "mp", split_axis=0, concat_axis=0, tiled=True)

    def spread(a):
        return over_mp(jnp.broadcast_to(a[None], (n,) + a.shape))

    hidden = pl.pallas_call(
        units_kernel,
        out_shape=jax.ShapeDtypeStruct((rows, units), BF16),
        in_specs=[VMEM] * 2,
        out_specs=VMEM,
        compiler_params=pltpu.CompilerParams(vmem_limit_bytes=24 << 20),
        cost_estimate=pl.CostEstimate(
            flops=2 * rows * units * width,
            bytes_accessed=2 * (units * width + rows * (units + width)),
            transcendentals=rows * units,
        ),
        name="units",
    )(spread(over_dp(out)), expert_weight)
    outs = pl.pallas_call(
        layers_kernel,
        out_shape=jax.ShapeDtypeStruct((n, rows, cols), BF16),
        in_specs=[VMEM] * 2,
        out_specs=VMEM,
        compiler_params=pltpu.CompilerParams(vmem_limit_bytes=24 << 20),
        cost_estimate=pl.CostEstimate(
            flops=2 * rows * units * towers * tile,
            bytes_accessed=2 * (units * towers * tile + rows * (units + towers * tile)),
            transcendentals=0,
        ),
        name="layers",
    )(hidden, tower_weight)
    total = pl.pallas_call(
        sum_kernel,
        out_shape=jax.ShapeDtypeStruct((rows // 8, 2, 8, cols // 2), BF16),
        in_specs=[VMEM],
        out_specs=VMEM,
        compiler_params=pltpu.CompilerParams(vmem_limit_bytes=16 << 20),
        name="total",
    )(over_mp(outs))
    task = lax.axis_index("task").astype(jnp.int32).reshape(1)
    back, side, task = lax.optimization_barrier((over_dp(total), side, task))

    z = pl.pallas_call(
        functools.partial(combine_kernel, experts, cap),
        out_shape=jax.ShapeDtypeStruct((n, count, cols), BF16),
        in_specs=[VMEM] * 3,
        out_specs=VMEM,
        compiler_params=pltpu.CompilerParams(vmem_limit_bytes=16 << 20),
        name="combine",
    )(ids, levels, back)
    zs = over_mp(z)

    pred = pl.pallas_call(
        functools.partial(predict_kernel, towers),
        out_shape=jax.ShapeDtypeStruct((towers, 1, count), F32),
        in_specs=[SMEM, VMEM, VMEM],
        out_specs=VMEM,
        compiler_params=pltpu.CompilerParams(vmem_limit_bytes=16 << 20),
        name="predict",
    )(task, side, zs)
    grad = pl.pallas_call(
        gradient_kernel,
        out_shape=jax.ShapeDtypeStruct((count, units), BF16),
        in_specs=[SMEM] + [VMEM] * 3,
        out_specs=VMEM,
        scratch_shapes=[pltpu.VMEM((count, units), F32)],
        compiler_params=pltpu.CompilerParams(vmem_limit_bytes=24 << 20),
        cost_estimate=pl.CostEstimate(
            flops=2 * count * units * towers * tile,
            bytes_accessed=2 * units * towers * tile,
            transcendentals=count * towers * tile,
        ),
        name="gradient",
    )(task, side, zs, tower_weight)
    pred = lax.all_to_all(pred, "task", split_axis=0, concat_axis=0, tiled=True)
    return pred.reshape(1, tasks * count), grad


def solution(mesh):
    return jax.shard_map(
        body,
        mesh=mesh,
        in_specs=(
            P(("dp", "task"), None),
            P(("dp", "task"), None),
            P(("dp", "task"), None),
            P("dp", None, "mp"),
            P(None, "mp", None),
            P("task", None),
            P("task", "dp"),
        ),
        out_specs=(P("task", "dp"), P(("dp", "task"), "mp")),
        check_vma=False,
    )
```

```python
import functools

import jax
import jax.numpy as jnp
from jax import lax
from jax.experimental import pallas as pl
from jax.experimental.pallas import tpu as pltpu
from jax.sharding import PartitionSpec as P

F32 = jnp.float32
BF16 = jnp.bfloat16
VMEM = pl.BlockSpec(memory_space=pltpu.VMEM)
SMEM = pl.BlockSpec(memory_space=pltpu.SMEM)
LANES = (((1,), (1,)), ((), ()))
ROWS = (((0,), (0,)), ((), ()))


def slot_rows(ids_ref, experts, pitch):
    top, count = ids_ref.shape
    earlier = (
        lax.broadcasted_iota(jnp.int32, (count, count), 0)
        < lax.broadcasted_iota(jnp.int32, (count, count), 1)
    ).astype(F32).astype(BF16)
    names = lax.broadcasted_iota(jnp.int32, (experts, count), 0)
    seen = jnp.zeros((experts, 1), F32)
    slots = []
    for k in range(top):
        row = ids_ref[k : k + 1, :]
        hit = (names == row).astype(F32)
        before = jnp.dot(hit.astype(BF16), earlier, preferred_element_type=F32)
        rank = jnp.sum(hit * (before + seen), axis=0, keepdims=True)
        seen = seen + jnp.sum(hit, axis=1, keepdims=True)
        slots.append(row * pitch + rank.astype(jnp.int32))
    return slots


def by_tiles(rows, out_ref):
    groups, halves, high, wide = out_ref.shape
    for h in range(halves):
        out_ref[:, h] = rows[:, h * wide : (h + 1) * wide].reshape(groups, high, wide).astype(BF16)


def sum_kernel(in_ref, out_ref):
    by_tiles(sum(in_ref[j].astype(F32) for j in range(in_ref.shape[0])), out_ref)


def dispatch_kernel(experts, pitch, col_ref, ids_ref, tok_ref, out_ref):
    slots = slot_rows(ids_ref, experts, pitch)
    count = ids_ref.shape[1]
    here = lax.broadcasted_iota(jnp.int32, (experts * pitch, count), 0)
    pick = functools.reduce(jnp.logical_or, [here == s for s in slots])
    pick = pick.astype(F32).astype(BF16)
    by_tiles(jnp.dot(pick, tok_ref[...], preferred_element_type=F32), out_ref)


def units_kernel(in_ref, w_ref, hid_ref):
    n, _, depth = in_ref.shape
    tile = 256

    @pl.loop(0, w_ref.shape[2] // tile)
    def _(c):
        cols = pl.ds(pl.multiple_of(c * tile, tile), tile)
        total = None
        for j in range(n):
            part = jnp.dot(
                in_ref[j], w_ref[0, j * depth : (j + 1) * depth, cols], preferred_element_type=F32
            )
            total = part if total is None else total + part
        hid_ref[:, cols] = (total / (1.0 + jnp.exp(-total))).astype(BF16)


def layers_kernel(hid_ref, tw_ref, out_ref):
    towers, _, tile = tw_ref.shape
    per = towers // out_ref.shape[0]
    for t in range(towers):
        out_ref[t // per, :, (t % per) * tile : (t % per + 1) * tile] = jnp.dot(
            hid_ref[...], tw_ref[t], preferred_element_type=F32
        ).astype(BF16)


def combine_kernel(experts, pitch, ids_ref, lev_ref, back_ref, out_ref):
    slots = slot_rows(ids_ref, experts, pitch)
    levels = lev_ref[...].astype(F32)
    gates = levels / jnp.sum(levels, axis=0, keepdims=True)
    here = lax.broadcasted_iota(jnp.int32, (experts * pitch, ids_ref.shape[1]), 0)
    share = sum(jnp.where(here == s, gates[k : k + 1, :], 0.0) for k, s in enumerate(slots))
    high = share.astype(BF16)
    low = (share - high.astype(F32)).astype(BF16)
    rows = back_ref[...]
    z = lax.dot_general(high, rows, ROWS, preferred_element_type=F32)
    z = z + lax.dot_general(low, rows, ROWS, preferred_element_type=F32)
    for j in range(out_ref.shape[0]):
        out_ref[j] = z.astype(BF16)


def from_tower(side_ref, me, t):
    return side_ref[pl.ds(jnp.bitwise_xor(me, t), 1), pl.ds(me, 1), :].reshape(1, -1)


def predict_kernel(towers, me_ref, side_ref, z_ref, pred_ref):
    me = me_ref[0]
    n, count, cols = z_ref.shape
    per = towers // n
    tile = cols // per
    lane = lax.broadcasted_iota(jnp.int32, (count, 128), 1)
    sums = jnp.zeros((count, 128), F32)
    for t in range(towers):
        z = z_ref[t // per, :, (t % per) * tile : (t % per + 1) * tile].astype(F32)
        out_vec = from_tower(side_ref, me, t)[:, -tile:]
        pred = jnp.sum(z / (1.0 + jnp.exp(-z)) * out_vec, axis=1, keepdims=True)
        sums = jnp.where(lane == t, pred, sums)
    sums = jnp.concatenate([sums, jnp.zeros((-count % 128, 128), F32)], axis=0)
    rows = jnp.transpose(sums)
    for t in range(towers):
        pred_ref[t] = rows[t : t + 1, :count]


def gradient_kernel(me_ref, side_ref, z_ref, tw_ref, grad_ref, acc_ref):
    me = me_ref[0]
    n, count, cols = z_ref.shape
    towers, _, tile = tw_ref.shape
    per = towers // n
    sides = [from_tower(side_ref, me, t) for t in range(towers)]
    cot = jnp.transpose(jnp.concatenate([v[:, :-tile] for v in sides], axis=0))[:count]
    for t in range(towers):
        z = z_ref[t // per, :, (t % per) * tile : (t % per + 1) * tile].astype(F32)
        sig = 1.0 / (1.0 + jnp.exp(-z))
        dz = cot[:, t : t + 1] * sides[t][:, -tile:] * sig * (1.0 + z * (1.0 - sig))
        part = lax.dot_general(dz.astype(BF16), tw_ref[t], LANES, preferred_element_type=F32)
        if t == 0:
            acc_ref[...] = part
        elif t < towers - 1:
            acc_ref[...] += part
        else:
            grad_ref[...] = (acc_ref[...] + part).astype(BF16)


def body(tokens, expert_ids, gate_levels, expert_weight, tower_weight, tower_out, cotangent):
    experts = lax.axis_size("dp")
    tasks = lax.axis_size("task")
    n = lax.axis_size("mp")
    count, top = expert_ids.shape
    width = tokens.shape[1]
    part = width // n
    towers, units, tile = tower_weight.shape
    cols = towers * tile // n
    cap = max(2, 5 * count * top // (4 * experts))
    rows = experts * cap
    me = lax.axis_index("mp").astype(jnp.int32).reshape(1)
    ids = expert_ids.T
    levels = gate_levels.T

    side = jnp.concatenate(
        [
            jnp.pad(cotangent.reshape(tasks, count), ((0, 0), (0, 256 - count))),
            jnp.broadcast_to(tower_out, (tasks, tile)),
        ],
        axis=1,
    )
    side = side[None]
    for bit in (1, 2, 4):
        other = lax.ppermute(side, "task", [(i, i ^ bit) for i in range(tasks)])
        side = jnp.concatenate([side, other], axis=0)

    out = pl.pallas_call(
        functools.partial(dispatch_kernel, experts, cap),
        out_shape=jax.ShapeDtypeStruct((rows // 8, 2, 8, part // 2), BF16),
        grid_spec=pltpu.PrefetchScalarGridSpec(
            num_scalar_prefetch=1,
            grid=(1,),
            in_specs=[
                pl.BlockSpec((top, count), lambda g, m: (0, 0)),
                pl.BlockSpec((count, part), lambda g, m: (0, m[0])),
            ],
            out_specs=pl.BlockSpec((rows // 8, 2, 8, part // 2), lambda g, m: (0, 0, 0, 0)),
        ),
        compiler_params=pltpu.CompilerParams(vmem_limit_bytes=16 << 20),
        name="dispatch",
    )(me, ids, tokens)

    def over_dp(a):
        a = a.transpose(0, 2, 1, 3).reshape(experts, cap, 2, a.shape[3])
        return lax.all_to_all(a, "dp", split_axis=0, concat_axis=0, tiled=True).reshape(rows, -1)

    def over_mp(a):
        return lax.all_to_all(a, "mp", split_axis=0, concat_axis=0, tiled=True)

    def spread(a):
        return over_mp(jnp.broadcast_to(a[None], (n,) + a.shape))

    hidden = pl.pallas_call(
        units_kernel,
        out_shape=jax.ShapeDtypeStruct((rows, units), BF16),
        in_specs=[VMEM] * 2,
        out_specs=VMEM,
        compiler_params=pltpu.CompilerParams(vmem_limit_bytes=24 << 20),
        cost_estimate=pl.CostEstimate(
            flops=2 * rows * units * width,
            bytes_accessed=2 * (units * width + rows * (units + width)),
            transcendentals=rows * units,
        ),
        name="units",
    )(spread(over_dp(out)), expert_weight)
    outs = pl.pallas_call(
        layers_kernel,
        out_shape=jax.ShapeDtypeStruct((n, rows, cols), BF16),
        in_specs=[VMEM] * 2,
        out_specs=VMEM,
        compiler_params=pltpu.CompilerParams(vmem_limit_bytes=24 << 20),
        cost_estimate=pl.CostEstimate(
            flops=2 * rows * units * towers * tile,
            bytes_accessed=2 * (units * towers * tile + rows * (units + towers * tile)),
            transcendentals=0,
        ),
        name="layers",
    )(hidden, tower_weight)
    total = pl.pallas_call(
        sum_kernel,
        out_shape=jax.ShapeDtypeStruct((rows // 8, 2, 8, cols // 2), BF16),
        in_specs=[VMEM],
        out_specs=VMEM,
        compiler_params=pltpu.CompilerParams(vmem_limit_bytes=16 << 20),
        name="total",
    )(over_mp(outs))
    task = lax.axis_index("task").astype(jnp.int32).reshape(1)
    back, side, task = lax.optimization_barrier((over_dp(total), side, task))

    z = pl.pallas_call(
        functools.partial(combine_kernel, experts, cap),
        out_shape=jax.ShapeDtypeStruct((n, count, cols), BF16),
        in_specs=[VMEM] * 3,
        out_specs=VMEM,
        compiler_params=pltpu.CompilerParams(vmem_limit_bytes=16 << 20),
        name="combine",
    )(ids, levels, back)
    zs = over_mp(z)

    pred = pl.pallas_call(
        functools.partial(predict_kernel, towers),
        out_shape=jax.ShapeDtypeStruct((towers, 1, count), F32),
        in_specs=[SMEM, VMEM, VMEM],
        out_specs=VMEM,
        compiler_params=pltpu.CompilerParams(vmem_limit_bytes=16 << 20),
        name="predict",
    )(task, side, zs)
    grad = pl.pallas_call(
        gradient_kernel,
        out_shape=jax.ShapeDtypeStruct((count, units), BF16),
        in_specs=[SMEM] + [VMEM] * 3,
        out_specs=VMEM,
        scratch_shapes=[pltpu.VMEM((count, units), F32)],
        compiler_params=pltpu.CompilerParams(vmem_limit_bytes=24 << 20),
        cost_estimate=pl.CostEstimate(
            flops=2 * count * units * towers * tile,
            bytes_accessed=2 * units * towers * tile,
            transcendentals=count * towers * tile,
        ),
        name="gradient",
    )(task, side, zs, tower_weight)
    pred = lax.all_to_all(pred, "task", split_axis=0, concat_axis=0, tiled=True)
    return pred.reshape(1, tasks * count), grad


def solution(mesh):
    return jax.shard_map(
        body,
        mesh=mesh,
        in_specs=(
            P(("dp", "task"), None),
            P(("dp", "task"), None),
            P(("dp", "task"), None),
            P("dp", None, "mp"),
            P(None, "mp", None),
            P("task", None),
            P("task", "dp"),
        ),
        out_specs=(P("task", "dp"), P(("dp", "task"), "mp")),
        check_vma=False,
    )
```

```python
import functools

import jax
import jax.numpy as jnp
from jax import lax
from jax.experimental import pallas as pl
from jax.experimental.pallas import tpu as pltpu
from jax.sharding import PartitionSpec as P

F32 = jnp.float32
BF16 = jnp.bfloat16
VMEM = pl.BlockSpec(memory_space=pltpu.VMEM)
SMEM = pl.BlockSpec(memory_space=pltpu.SMEM)
LANES = (((1,), (1,)), ((), ()))
ROWS = (((0,), (0,)), ((), ()))


def slot_rows(ids_ref, experts, pitch):
    top, count = ids_ref.shape
    earlier = (
        lax.broadcasted_iota(jnp.int32, (count, count), 0)
        < lax.broadcasted_iota(jnp.int32, (count, count), 1)
    ).astype(F32).astype(BF16)
    names = lax.broadcasted_iota(jnp.int32, (experts, count), 0)
    seen = jnp.zeros((experts, 1), F32)
    slots = []
    for k in range(top):
        row = ids_ref[k : k + 1, :]
        hit = (names == row).astype(F32)
        before = jnp.dot(hit.astype(BF16), earlier, preferred_element_type=F32)
        rank = jnp.sum(hit * (before + seen), axis=0, keepdims=True)
        seen = seen + jnp.sum(hit, axis=1, keepdims=True)
        slots.append(row * pitch + rank.astype(jnp.int32))
    return slots


def by_tiles(rows, out_ref):
    groups, halves, high, wide = out_ref.shape
    for h in range(halves):
        out_ref[:, h] = rows[:, h * wide : (h + 1) * wide].reshape(groups, high, wide).astype(BF16)


def sum_kernel(in_ref, out_ref):
    by_tiles(sum(in_ref[j].astype(F32) for j in range(in_ref.shape[0])), out_ref)


def dispatch_kernel(experts, pitch, ids_ref, tok_ref, out_ref):
    slots = slot_rows(ids_ref, experts, pitch)
    count = ids_ref.shape[1]
    here = lax.broadcasted_iota(jnp.int32, (experts * pitch, count), 0)
    pick = functools.reduce(jnp.logical_or, [here == s for s in slots])
    pick = pick.astype(F32).astype(BF16)
    by_tiles(jnp.dot(pick, tok_ref[...], preferred_element_type=F32), out_ref)


def units_kernel(in_ref, w_ref, hid_ref):
    n, _, depth = in_ref.shape
    tile = 256

    @pl.loop(0, w_ref.shape[2] // tile)
    def _(c):
        cols = pl.ds(pl.multiple_of(c * tile, tile), tile)
        total = None
        for j in range(n):
            part = jnp.dot(
                in_ref[j], w_ref[0, j * depth : (j + 1) * depth, cols], preferred_element_type=F32
            )
            total = part if total is None else total + part
        hid_ref[:, cols] = (total / (1.0 + jnp.exp(-total))).astype(BF16)


def layers_kernel(hid_ref, tw_ref, out_ref):
    towers, _, tile = tw_ref.shape
    per = towers // out_ref.shape[0]
    for t in range(towers):
        out_ref[t // per, :, (t % per) * tile : (t % per + 1) * tile] = jnp.dot(
            hid_ref[...], tw_ref[t], preferred_element_type=F32
        ).astype(BF16)


def combine_kernel(experts, pitch, ids_ref, lev_ref, back_ref, out_ref):
    slots = slot_rows(ids_ref, experts, pitch)
    levels = lev_ref[...].astype(F32)
    gates = levels / jnp.sum(levels, axis=0, keepdims=True)
    here = lax.broadcasted_iota(jnp.int32, (experts * pitch, ids_ref.shape[1]), 0)
    share = sum(jnp.where(here == s, gates[k : k + 1, :], 0.0) for k, s in enumerate(slots))
    high = share.astype(BF16)
    low = (share - high.astype(F32)).astype(BF16)
    rows = back_ref[...]
    z = lax.dot_general(high, rows, ROWS, preferred_element_type=F32)
    z = z + lax.dot_general(low, rows, ROWS, preferred_element_type=F32)
    for j in range(out_ref.shape[0]):
        out_ref[j] = z.astype(BF16)


def from_tower(side_ref, me, t):
    return side_ref[pl.ds(jnp.bitwise_xor(me, t), 1), pl.ds(me, 1), :].reshape(1, -1)


def predict_kernel(towers, me_ref, side_ref, z_ref, pred_ref):
    me = me_ref[0]
    n, count, cols = z_ref.shape
    per = towers // n
    tile = cols // per
    lane = lax.broadcasted_iota(jnp.int32, (count, 128), 1)
    sums = jnp.zeros((count, 128), F32)
    for t in range(towers):
        z = z_ref[t // per, :, (t % per) * tile : (t % per + 1) * tile].astype(F32)
        out_vec = from_tower(side_ref, me, t)[:, -tile:]
        pred = jnp.sum(z / (1.0 + jnp.exp(-z)) * out_vec, axis=1, keepdims=True)
        sums = jnp.where(lane == t, pred, sums)
    sums = jnp.concatenate([sums, jnp.zeros((-count % 128, 128), F32)], axis=0)
    rows = jnp.transpose(sums)
    for t in range(towers):
        pred_ref[t] = rows[t : t + 1, :count]


def gradient_kernel(me_ref, side_ref, z_ref, tw_ref, grad_ref, acc_ref):
    me = me_ref[0]
    n, count, cols = z_ref.shape
    towers, _, tile = tw_ref.shape
    per = towers // n
    sides = [from_tower(side_ref, me, t) for t in range(towers)]
    cot = jnp.transpose(jnp.concatenate([v[:, :-tile] for v in sides], axis=0))[:count]
    for t in range(towers):
        z = z_ref[t // per, :, (t % per) * tile : (t % per + 1) * tile].astype(F32)
        sig = 1.0 / (1.0 + jnp.exp(-z))
        dz = cot[:, t : t + 1] * sides[t][:, -tile:] * sig * (1.0 + z * (1.0 - sig))
        part = lax.dot_general(dz.astype(BF16), tw_ref[t], LANES, preferred_element_type=F32)
        if t == 0:
            acc_ref[...] = part
        elif t < towers - 1:
            acc_ref[...] += part
        else:
            grad_ref[...] = (acc_ref[...] + part).astype(BF16)


def body(tokens, expert_ids, gate_levels, expert_weight, tower_weight, tower_out, cotangent):
    experts = lax.axis_size("dp")
    tasks = lax.axis_size("task")
    n = lax.axis_size("mp")
    count, top = expert_ids.shape
    width = tokens.shape[1]
    part = width // n
    towers, units, tile = tower_weight.shape
    cols = towers * tile // n
    cap = max(2, 5 * count * top // (4 * experts))
    rows = experts * cap
    ids = expert_ids.T
    levels = gate_levels.T

    side = jnp.concatenate(
        [
            jnp.pad(cotangent.reshape(tasks, count), ((0, 0), (0, 256 - count))),
            jnp.broadcast_to(tower_out, (tasks, tile)),
        ],
        axis=1,
    )
    side = side[None]
    for bit in (1, 2, 4):
        other = lax.ppermute(side, "task", [(i, i ^ bit) for i in range(tasks)])
        side = jnp.concatenate([side, other], axis=0)

    out = pl.pallas_call(
        functools.partial(dispatch_kernel, experts, cap),
        out_shape=jax.ShapeDtypeStruct((rows // 8, 2, 8, part // 2), BF16),
        in_specs=[VMEM] * 2,
        out_specs=VMEM,
        compiler_params=pltpu.CompilerParams(vmem_limit_bytes=16 << 20),
        name="dispatch",
    )(ids, lax.dynamic_slice_in_dim(tokens, lax.axis_index("mp") * part, part, axis=1))

    def over_dp(a):
        a = a.transpose(0, 2, 1, 3).reshape(experts, cap, 2, a.shape[3])
        return lax.all_to_all(a, "dp", split_axis=0, concat_axis=0, tiled=True).reshape(rows, -1)

    def over_mp(a):
        return lax.all_to_all(a, "mp", split_axis=0, concat_axis=0, tiled=True)

    def spread(a):
        return over_mp(jnp.broadcast_to(a[None], (n,) + a.shape))

    hidden = pl.pallas_call(
        units_kernel,
        out_shape=jax.ShapeDtypeStruct((rows, units), BF16),
        in_specs=[VMEM] * 2,
        out_specs=VMEM,
        compiler_params=pltpu.CompilerParams(vmem_limit_bytes=24 << 20),
        cost_estimate=pl.CostEstimate(
            flops=2 * rows * units * width,
            bytes_accessed=2 * (units * width + rows * (units + width)),
            transcendentals=rows * units,
        ),
        name="units",
    )(spread(over_dp(out)), expert_weight)
    outs = pl.pallas_call(
        layers_kernel,
        out_shape=jax.ShapeDtypeStruct((n, rows, cols), BF16),
        in_specs=[VMEM] * 2,
        out_specs=VMEM,
        compiler_params=pltpu.CompilerParams(vmem_limit_bytes=24 << 20),
        cost_estimate=pl.CostEstimate(
            flops=2 * rows * units * towers * tile,
            bytes_accessed=2 * (units * towers * tile + rows * (units + towers * tile)),
            transcendentals=0,
        ),
        name="layers",
    )(hidden, tower_weight)
    total = pl.pallas_call(
        sum_kernel,
        out_shape=jax.ShapeDtypeStruct((rows // 8, 2, 8, cols // 2), BF16),
        in_specs=[VMEM],
        out_specs=VMEM,
        compiler_params=pltpu.CompilerParams(vmem_limit_bytes=16 << 20),
        name="total",
    )(over_mp(outs))
    task = lax.axis_index("task").astype(jnp.int32).reshape(1)
    back, side, task = lax.optimization_barrier((over_dp(total), side, task))

    z = pl.pallas_call(
        functools.partial(combine_kernel, experts, cap),
        out_shape=jax.ShapeDtypeStruct((n, count, cols), BF16),
        in_specs=[VMEM] * 3,
        out_specs=VMEM,
        compiler_params=pltpu.CompilerParams(vmem_limit_bytes=16 << 20),
        name="combine",
    )(ids, levels, back)
    zs = over_mp(z)

    pred = pl.pallas_call(
        functools.partial(predict_kernel, towers),
        out_shape=jax.ShapeDtypeStruct((towers, 1, count), F32),
        in_specs=[SMEM, VMEM, VMEM],
        out_specs=VMEM,
        compiler_params=pltpu.CompilerParams(vmem_limit_bytes=16 << 20),
        name="predict",
    )(task, side, zs)
    grad = pl.pallas_call(
        gradient_kernel,
        out_shape=jax.ShapeDtypeStruct((count, units), BF16),
        in_specs=[SMEM] + [VMEM] * 3,
        out_specs=VMEM,
        scratch_shapes=[pltpu.VMEM((count, units), F32)],
        compiler_params=pltpu.CompilerParams(vmem_limit_bytes=24 << 20),
        cost_estimate=pl.CostEstimate(
            flops=2 * count * units * towers * tile,
            bytes_accessed=2 * units * towers * tile,
            transcendentals=count * towers * tile,
        ),
        name="gradient",
    )(task, side, zs, tower_weight)
    pred = lax.all_to_all(pred, "task", split_axis=0, concat_axis=0, tiled=True)
    return pred.reshape(1, tasks * count), grad


def solution(mesh):
    return jax.shard_map(
        body,
        mesh=mesh,
        in_specs=(
            P(("dp", "task"), None),
            P(("dp", "task"), None),
            P(("dp", "task"), None),
            P("dp", None, "mp"),
            P(None, "mp", None),
            P("task", None),
            P("task", "dp"),
        ),
        out_specs=(P("task", "dp"), P(("dp", "task"), "mp")),
        check_vma=False,
    )
```

```python
import functools

import jax
import jax.numpy as jnp
from jax import lax
from jax.experimental import pallas as pl
from jax.experimental.pallas import tpu as pltpu
from jax.sharding import PartitionSpec as P

F32 = jnp.float32
BF16 = jnp.bfloat16
VMEM = pl.BlockSpec(memory_space=pltpu.VMEM)
SMEM = pl.BlockSpec(memory_space=pltpu.SMEM)
LANES = (((1,), (1,)), ((), ()))
ROWS = (((0,), (0,)), ((), ()))


def slot_rows(ids_ref, experts, pitch):
    top, count = ids_ref.shape
    earlier = (
        lax.broadcasted_iota(jnp.int32, (count, count), 0)
        < lax.broadcasted_iota(jnp.int32, (count, count), 1)
    ).astype(F32).astype(BF16)
    names = lax.broadcasted_iota(jnp.int32, (experts, count), 0)
    seen = jnp.zeros((experts, 1), F32)
    slots = []
    for k in range(top):
        row = ids_ref[k : k + 1, :]
        hit = (names == row).astype(F32)
        before = jnp.dot(hit.astype(BF16), earlier, preferred_element_type=F32)
        rank = jnp.sum(hit * (before + seen), axis=0, keepdims=True)
        seen = seen + jnp.sum(hit, axis=1, keepdims=True)
        slots.append(row * pitch + rank.astype(jnp.int32))
    return slots


def by_tiles(rows, out_ref):
    groups, halves, high, wide = out_ref.shape
    for h in range(halves):
        out_ref[:, h] = rows[:, h * wide : (h + 1) * wide].reshape(groups, high, wide).astype(BF16)


def sum_kernel(in_ref, out_ref):
    by_tiles(sum(in_ref[j].astype(F32) for j in range(in_ref.shape[0])), out_ref)


def dispatch_kernel(experts, pitch, col_ref, ids_ref, tok_ref, out_ref):
    slots = slot_rows(ids_ref, experts, pitch)
    count = ids_ref.shape[1]
    here = lax.broadcasted_iota(jnp.int32, (experts * pitch, count), 0)
    pick = functools.reduce(jnp.logical_or, [here == s for s in slots])
    pick = pick.astype(F32).astype(BF16)
    by_tiles(jnp.dot(pick, tok_ref[...], preferred_element_type=F32), out_ref)


def units_kernel(in_ref, w_ref, hid_ref):
    n, _, depth = in_ref.shape
    tile = 256

    for c in range(w_ref.shape[2] // tile):
        cols = slice(c * tile, (c + 1) * tile)
        total = None
        for j in range(n):
            part = jnp.dot(
                in_ref[j], w_ref[0, j * depth : (j + 1) * depth, cols], preferred_element_type=F32
            )
            total = part if total is None else total + part
        hid_ref[:, cols] = (total / (1.0 + jnp.exp(-total))).astype(BF16)


def layers_kernel(hid_ref, tw_ref, out_ref):
    towers, _, tile = tw_ref.shape
    per = towers // out_ref.shape[0]
    for t in range(towers):
        out_ref[t // per, :, (t % per) * tile : (t % per + 1) * tile] = jnp.dot(
            hid_ref[...], tw_ref[t], preferred_element_type=F32
        ).astype(BF16)


def combine_kernel(experts, pitch, ids_ref, lev_ref, back_ref, out_ref):
    slots = slot_rows(ids_ref, experts, pitch)
    levels = lev_ref[...].astype(F32)
    gates = levels / jnp.sum(levels, axis=0, keepdims=True)
    here = lax.broadcasted_iota(jnp.int32, (experts * pitch, ids_ref.shape[1]), 0)
    share = sum(jnp.where(here == s, gates[k : k + 1, :], 0.0) for k, s in enumerate(slots))
    high = share.astype(BF16)
    low = (share - high.astype(F32)).astype(BF16)
    rows = back_ref[...]
    z = lax.dot_general(high, rows, ROWS, preferred_element_type=F32)
    z = z + lax.dot_general(low, rows, ROWS, preferred_element_type=F32)
    for j in range(out_ref.shape[0]):
        out_ref[j] = z.astype(BF16)


def from_tower(side_ref, me, t):
    return side_ref[pl.ds(jnp.bitwise_xor(me, t), 1), pl.ds(me, 1), :].reshape(1, -1)


def predict_kernel(towers, me_ref, side_ref, z_ref, pred_ref):
    me = me_ref[0]
    n, count, cols = z_ref.shape
    per = towers // n
    tile = cols // per
    lane = lax.broadcasted_iota(jnp.int32, (count, 128), 1)
    sums = jnp.zeros((count, 128), F32)
    for t in range(towers):
        z = z_ref[t // per, :, (t % per) * tile : (t % per + 1) * tile].astype(F32)
        out_vec = from_tower(side_ref, me, t)[:, -tile:]
        pred = jnp.sum(z / (1.0 + jnp.exp(-z)) * out_vec, axis=1, keepdims=True)
        sums = jnp.where(lane == t, pred, sums)
    sums = jnp.concatenate([sums, jnp.zeros((-count % 128, 128), F32)], axis=0)
    rows = jnp.transpose(sums)
    for t in range(towers):
        pred_ref[t] = rows[t : t + 1, :count]


def gradient_kernel(me_ref, side_ref, z_ref, tw_ref, grad_ref, acc_ref):
    me = me_ref[0]
    n, count, cols = z_ref.shape
    towers, _, tile = tw_ref.shape
    per = towers // n
    sides = [from_tower(side_ref, me, t) for t in range(towers)]
    cot = jnp.transpose(jnp.concatenate([v[:, :-tile] for v in sides], axis=0))[:count]
    for t in range(towers):
        z = z_ref[t // per, :, (t % per) * tile : (t % per + 1) * tile].astype(F32)
        sig = 1.0 / (1.0 + jnp.exp(-z))
        dz = cot[:, t : t + 1] * sides[t][:, -tile:] * sig * (1.0 + z * (1.0 - sig))
        part = lax.dot_general(dz.astype(BF16), tw_ref[t], LANES, preferred_element_type=F32)
        if t == 0:
            acc_ref[...] = part
        elif t < towers - 1:
            acc_ref[...] += part
        else:
            grad_ref[...] = (acc_ref[...] + part).astype(BF16)


def body(tokens, expert_ids, gate_levels, expert_weight, tower_weight, tower_out, cotangent):
    experts = lax.axis_size("dp")
    tasks = lax.axis_size("task")
    n = lax.axis_size("mp")
    count, top = expert_ids.shape
    width = tokens.shape[1]
    part = width // n
    towers, units, tile = tower_weight.shape
    cols = towers * tile // n
    cap = max(2, 5 * count * top // (4 * experts))
    rows = experts * cap
    me = lax.axis_index("mp").astype(jnp.int32).reshape(1)
    ids = expert_ids.T
    levels = gate_levels.T

    side = jnp.concatenate(
        [
            jnp.pad(cotangent.reshape(tasks, count), ((0, 0), (0, 256 - count))),
            jnp.broadcast_to(tower_out, (tasks, tile)),
        ],
        axis=1,
    )
    side = side[None]
    for bit in (1, 2, 4):
        other = lax.ppermute(side, "task", [(i, i ^ bit) for i in range(tasks)])
        side = jnp.concatenate([side, other], axis=0)

    out = pl.pallas_call(
        functools.partial(dispatch_kernel, experts, cap),
        out_shape=jax.ShapeDtypeStruct((rows // 8, 2, 8, part // 2), BF16),
        grid_spec=pltpu.PrefetchScalarGridSpec(
            num_scalar_prefetch=1,
            grid=(1,),
            in_specs=[
                pl.BlockSpec((top, count), lambda g, m: (0, 0)),
                pl.BlockSpec((count, part), lambda g, m: (0, m[0])),
            ],
            out_specs=pl.BlockSpec((rows // 8, 2, 8, part // 2), lambda g, m: (0, 0, 0, 0)),
        ),
        compiler_params=pltpu.CompilerParams(vmem_limit_bytes=16 << 20),
        name="dispatch",
    )(me, ids, tokens)

    def over_dp(a):
        a = a.transpose(0, 2, 1, 3).reshape(experts, cap, 2, a.shape[3])
        return lax.all_to_all(a, "dp", split_axis=0, concat_axis=0, tiled=True).reshape(rows, -1)

    def over_mp(a):
        return lax.all_to_all(a, "mp", split_axis=0, concat_axis=0, tiled=True)

    def spread(a):
        return over_mp(jnp.broadcast_to(a[None], (n,) + a.shape))

    hidden = pl.pallas_call(
        units_kernel,
        out_shape=jax.ShapeDtypeStruct((rows, units), BF16),
        in_specs=[VMEM] * 2,
        out_specs=VMEM,
        compiler_params=pltpu.CompilerParams(vmem_limit_bytes=24 << 20),
        cost_estimate=pl.CostEstimate(
            flops=2 * rows * units * width,
            bytes_accessed=2 * (units * width + rows * (units + width)),
            transcendentals=rows * units,
        ),
        name="units",
    )(spread(over_dp(out)), expert_weight)
    outs = pl.pallas_call(
        layers_kernel,
        out_shape=jax.ShapeDtypeStruct((n, rows, cols), BF16),
        in_specs=[VMEM] * 2,
        out_specs=VMEM,
        compiler_params=pltpu.CompilerParams(vmem_limit_bytes=24 << 20),
        cost_estimate=pl.CostEstimate(
            flops=2 * rows * units * towers * tile,
            bytes_accessed=2 * (units * towers * tile + rows * (units + towers * tile)),
            transcendentals=0,
        ),
        name="layers",
    )(hidden, tower_weight)
    total = pl.pallas_call(
        sum_kernel,
        out_shape=jax.ShapeDtypeStruct((rows // 8, 2, 8, cols // 2), BF16),
        in_specs=[VMEM],
        out_specs=VMEM,
        compiler_params=pltpu.CompilerParams(vmem_limit_bytes=16 << 20),
        name="total",
    )(over_mp(outs))
    task = lax.axis_index("task").astype(jnp.int32).reshape(1)
    back, side, task = lax.optimization_barrier((over_dp(total), side, task))

    z = pl.pallas_call(
        functools.partial(combine_kernel, experts, cap),
        out_shape=jax.ShapeDtypeStruct((n, count, cols), BF16),
        in_specs=[VMEM] * 3,
        out_specs=VMEM,
        compiler_params=pltpu.CompilerParams(vmem_limit_bytes=16 << 20),
        name="combine",
    )(ids, levels, back)
    zs = over_mp(z)

    pred = pl.pallas_call(
        functools.partial(predict_kernel, towers),
        out_shape=jax.ShapeDtypeStruct((towers, 1, count), F32),
        in_specs=[SMEM, VMEM, VMEM],
        out_specs=VMEM,
        compiler_params=pltpu.CompilerParams(vmem_limit_bytes=16 << 20),
        name="predict",
    )(task, side, zs)
    grad = pl.pallas_call(
        gradient_kernel,
        out_shape=jax.ShapeDtypeStruct((count, units), BF16),
        in_specs=[SMEM] + [VMEM] * 3,
        out_specs=VMEM,
        scratch_shapes=[pltpu.VMEM((count, units), F32)],
        compiler_params=pltpu.CompilerParams(vmem_limit_bytes=24 << 20),
        cost_estimate=pl.CostEstimate(
            flops=2 * count * units * towers * tile,
            bytes_accessed=2 * units * towers * tile,
            transcendentals=count * towers * tile,
        ),
        name="gradient",
    )(task, side, zs, tower_weight)
    pred = lax.all_to_all(pred, "task", split_axis=0, concat_axis=0, tiled=True)
    return pred.reshape(1, tasks * count), grad


def solution(mesh):
    return jax.shard_map(
        body,
        mesh=mesh,
        in_specs=(
            P(("dp", "task"), None),
            P(("dp", "task"), None),
            P(("dp", "task"), None),
            P("dp", None, "mp"),
            P(None, "mp", None),
            P("task", None),
            P("task", "dp"),
        ),
        out_specs=(P("task", "dp"), P(("dp", "task"), "mp")),
        check_vma=False,
    )
```
